32 devices in a mesh: gx: 4 (over y, x), gy: 8 (over z, core).
Axes of the slice: x: 2, y: 2, z: 4, core: 2. Of those that a mesh axis runs over, the one named last changes fastest.
Arguments:
- stream_in: bfloat16 [256, 4096], P('gx', 'gy'), may hold values from -6 to 6
- queries: bfloat16 [256, 4096], P('gx'), may hold values from -28 to 28
- suffix_keys: bfloat16 [256, 1024], P('gx'), may hold values from -6 to 6
- suffix_values: bfloat16 [256, 1024], P('gx'), may hold values from -6 to 6
- prefix_keys: bfloat16 [4, 4096, 1024], P('gx', 'gy'), may hold values from -16 to 16
- prefix_values: bfloat16 [4, 4096, 1024], P('gx', 'gy'), may hold values from -6 to 6
- lengths: int32 [4, 4], P('gx'), may hold values from 1 to 32, 64 in all within a row
- req_group: int32 [4, 4], P('gx'), may hold values from 0 to 2
- owners: int32 [3], replicated, may hold values from 0 to 3, as said below
- out_proj: bfloat16 [4096, 4096], P(None, 'gy'), may hold values from -0.09375 to 0.09375
- norm_gain: float32 [4096], P('gy'), may hold values from 0.1 to 1.9
- w_gate: bfloat16 [8, 4096, 8192], P(None, 'gy', 'gx'), may hold values from -0.09375 to 0.09375
- w_up: bfloat16 [8, 4096, 8192], P(None, 'gy', 'gx'), may hold values from -0.09375 to 0.09375
- w_down: bfloat16 [8, 8192, 4096], P(None, 'gx', 'gy'), may hold values from -0.0625 to 0.0625
- routes: int32 [256, 2], replicated, may hold values from 0 to 7, all different within a row; in each aligned block of 256 rows (0 to 255, 256 to 511, ...) at most 96 rows name the same one
- route_logits: float32 [256, 2], replicated, may hold values from -6 to 6
Outputs:
- layer_out: bfloat16 [256, 4096], P('gx', 'gy')
The draws below stay inside these ranges and needn't reach their ends.
Inputs may be any that keep to these rules, and one draw needn't show every extreme that they name: `owners`: the 3 entries are different. `routes`: the two entries of a row differ; at most 96 rows name one expert. `lengths`: each row sums to 64; its largest entry is 32.
All inputs are finite; a program needn't handle non-finite values.
Results may differ from the reference program's by a relative error of at most 0.008.
Values may be sent and summed in bfloat16 or wider, within the bound.
No kernel may reach another device: no remote copies, remote signals or barrier semaphores. Data moves between devices by JAX's collectives and lax.ppermute only.
A program may use at most 192 MiB of HBM per device.

```python
import math
from functools import reduce
import jax
import jax.numpy as jnp
import numpy as np
from jax import lax

D = 4096
HEADS = 32
KVH = 8
HD = 128
EXPERTS = 8
TOPK = 2
FF = 8192
GROUPS = 3
REQ_DEV = 4
PREFIX = 4096
TOK_DEV = 64
TOKENS = 256
CAP = 96
LMAX = 32
N_GX = 4


def shared_direction(key):
    flips = jax.random.bernoulli(jax.random.fold_in(key, 101), 0.5, (HD,))
    return jnp.where(flips, 1.0, -1.0).astype(jnp.float32)


def draw_queries(key, part):
    base = 3.0 * jnp.clip(jax.random.normal(jax.random.fold_in(key, 1), (TOKENS, HEADS * HD), jnp.float32), -4.0, 4.0)
    direction = shared_direction(key)
    rows_all = jnp.arange(TOKENS)
    strength = jnp.where(rows_all % 3 == 0, 8.0, jnp.where(rows_all % 3 == 1, 11.0, 15.0))
    picked = rows_all % 37 == 5
    aligned = strength[:, None] * jnp.tile(direction, HEADS)[None, :]
    return jnp.where(picked[:, None], aligned, base).astype(jnp.bfloat16)


def draw_prefix_keys(key, part):
    base = jnp.clip(jax.random.normal(jax.random.fold_in(key, 2), (N_GX, PREFIX, KVH * HD), jnp.float32), -4.0, 4.0)
    direction = jnp.tile(shared_direction(key), KVH)
    places = jnp.arange(PREFIX, dtype=jnp.int32)
    first_place = jax.random.randint(jax.random.fold_in(key, 4), (N_GX,), 2, PREFIX, dtype=jnp.int32)
    offset = jax.random.randint(jax.random.fold_in(key, 5), (N_GX,), 1, PREFIX - 2, dtype=jnp.int32)
    second_place = 2 + (first_place - 2 + offset) % (PREFIX - 2)
    is_first = places[None, :] == first_place[:, None]
    is_second = places[None, :] == second_place[:, None]
    second_level = 3.96875 if HD <= 32 else 3.984375
    levels = jnp.where(is_first, 4.0, second_level)
    aligned = levels[:, :, None] * direction[None, None, :]
    return jnp.where((is_first | is_second)[:, :, None], aligned, base).astype(jnp.bfloat16)


def draw_owners(key, part):
    return jax.random.permutation(jax.random.fold_in(key, 3), N_GX)[:GROUPS].astype(jnp.int32)


def touch_ends(values, stream_key, least, high):
    longest = values.shape.index(max(values.shape))
    spots = []
    for shift in (0, 1):
        where = [jax.random.randint(jax.random.fold_in(stream_key, axis), (), 0, length) for axis, length in enumerate(values.shape)]
        where[longest] = (where[longest] + shift) % values.shape[longest]
        spots.append(tuple(where))
    return values.at[spots[0]].set(least).at[spots[1]].set(high)


def block_levels(key, extent, split, smallest, largest):
    factor_of = 1.0
    for axis_at, shards_of in split:
        heights = jax.random.uniform(jax.random.fold_in(jax.random.fold_in(key, 6), axis_at), (shards_of,), jnp.float32, smallest / len(split), largest / len(split))
        factor_of = factor_of * jnp.repeat(jnp.exp(heights), extent[axis_at] // shards_of).reshape((-1,) + (1,) * (len(extent) - 1 - axis_at))
    return factor_of


def split_up(number_of, total, limit, lean):
    weights = [(1 << 20) // math.isqrt(standing ** lean) + 1 for standing in range(2, number_of + 1)]
    surplus, given = total - limit - (number_of - 1), [1] * (number_of - 1)
    while surplus > 0:
        movable = [i for i in range(number_of - 1) if given[i] < limit]
        mass, budget = sum([weights[i] for i in movable]), surplus
        for i in movable:
            more = min(limit - given[i], max(1, budget * weights[i] // mass), surplus)
            given[i] = given[i] + more
            surplus = surplus - more
    return np.array([limit] + given)


def uneven(stream_key, number_of, total, most, skew):
    if number_of == 2:
        one = jax.random.randint(stream_key, (), max(1, total - most), min(most, total - 1) + 1)
        return jnp.stack([one, total - one])
    sizes = jnp.asarray(split_up(number_of, total, most, skew), jnp.int32)
    couples = (number_of - 1) // 2
    donor, receiver = sizes[1:1 + 2 * couples:2], sizes[2:2 + 2 * couples:2]
    room = jnp.minimum(donor - 1, most - receiver)
    moved = jax.random.randint(jax.random.fold_in(stream_key, 1), (couples,), 0, 1 << 20) % (room + 1)
    sizes = sizes.at[1:1 + 2 * couples:2].set(donor - moved).at[2:2 + 2 * couples:2].set(receiver + moved)
    return sizes[jax.random.permutation(jax.random.fold_in(stream_key, 2), number_of)]


def shared_out(key, own, number, rows, number_of, top, limit, slope):
    ranking = jax.random.permutation(key, number_of)
    packed, usual = load_shares(number_of, rows * top, limit, slope, True), load_shares(number_of, rows * top, limit, slope, False)
    places = jnp.arange(number_of)

    def named(sizes, rotation):
        used = int((sizes > 0).sum())
        fixed = max(1, used // 4)
        moved = fixed + (places - fixed + rotation * (used - fixed)) % max(1, number_of - fixed)
        return jnp.zeros((number_of,), jnp.int32).at[ranking[jnp.where(places < fixed, places, moved)]].set(jnp.asarray(sizes, jnp.int32))

    sizes = jnp.where(number % 4 == 0, named(packed, number // 4), named(usual, number - number // 4 - 1))
    mixed = jax.random.permutation(jax.random.fold_in(own, 3), number_of)
    giver, sink = mixed[0:number_of // 2 * 2:2], mixed[1:number_of // 2 * 2:2]
    margin = jnp.minimum(sizes[giver] - 1, limit - sizes[sink]) // 2
    margin = jnp.where((giver == ranking[0]) | (sink == ranking[0]) | (sizes[sink] == 0), 0, jnp.maximum(margin, 0))
    moved = jax.random.randint(jax.random.fold_in(own, 4), (number_of // 2,), 0, 1 << 20) % (margin + 1)
    sizes = sizes.at[giver].add(-moved).at[sink].add(moved)
    labels = jnp.searchsorted(jnp.cumsum(sizes), jnp.arange(rows * top), side="right").astype(jnp.int32)
    table = labels.reshape(top, rows).T
    table = table[jax.random.permutation(jax.random.fold_in(own, 1), rows)]
    rotation = jax.random.randint(jax.random.fold_in(own, 2), (rows, 1), 0, top)
    return jnp.take_along_axis(table, (jnp.arange(top)[None, :] + rotation) % top, axis=1)


def load_shares(count, total, limit, slope, full):
    portions = [(1 << 20) // math.isqrt(grade ** slope) + 1 for grade in range(1, count + 1)]
    largest = limit if full else min(limit, max(-(-total // count), total * portions[0] // sum(portions)))
    least = 1 if total - largest >= count - 1 else 0
    given, surplus = [largest] + [least] * (count - 1), total - largest - least * (count - 1)
    while surplus > 0:
        candidates = [i for i in range(1, count) if given[i] < largest] or [i for i in range(1, count) if given[i] < limit]
        whole, budget = sum([portions[i] for i in candidates]), surplus
        for i in candidates:
            addition = min(limit - given[i], max(1, budget * portions[i] // whole), surplus)
            given[i] = given[i] + addition
            surplus = surplus - addition
    return np.array(given)


def normal_values(rng, shape, scale, bound, cuts=(), kind=jnp.bfloat16):
    values = scale * jax.random.normal(rng, shape, jnp.float32)
    if cuts:
        values = values * block_levels(rng, shape, cuts, -0.22, 0.18)
    return jnp.clip(values, -bound, bound).astype(kind)


def setup_inputs(seed: int = 0) -> dict:
    key_list = jax.random.split(jax.random.key(seed), 17)
    stream_in = normal_values(key_list[0], (TOKENS, D), 1.0, 6.0, ((0, 4), (1, 8)))
    queries = draw_queries(jax.random.fold_in(key_list[16], 71), 0)
    suffix_keys = normal_values(key_list[2], (TOKENS, KVH * HD), 1.0, 6.0, ((0, 4),))
    suffix_values = normal_values(key_list[3], (TOKENS, KVH * HD), 1.0, 6.0, ((0, 4),))
    prefix_keys = draw_prefix_keys(jax.random.fold_in(key_list[16], 71), 0)
    prefix_values = normal_values(key_list[5], (N_GX, PREFIX, KVH * HD), 1.0, 6.0, ((0, 4), (1, 8)))
    lengths = jax.vmap(lambda own: uneven(own, REQ_DEV, TOK_DEV, LMAX, 2))(jax.random.split(key_list[6], N_GX)).reshape((N_GX, REQ_DEV)).astype(jnp.int32)
    req_group = touch_ends(jax.random.randint(key_list[7], (N_GX, REQ_DEV), 0, GROUPS), jax.random.fold_in(key_list[7], 1), 0, GROUPS - 1).astype(jnp.int32)
    owners = draw_owners(jax.random.fold_in(key_list[16], 71), 0)
    out_proj = normal_values(key_list[9], (HEADS * HD, D), (HEADS * HD) ** -0.5, 0.09375, ((1, 8),))
    norm_gain = jnp.clip(1.0 + 0.18 * jax.random.normal(key_list[10], (D,), jnp.float32), 0.1, 1.9)
    w_gate = normal_values(key_list[11], (EXPERTS, D, FF), D ** -0.5, 0.09375, ((1, 8), (2, 4)))
    w_up = normal_values(key_list[12], (EXPERTS, D, FF), D ** -0.5, 0.09375, ((1, 8), (2, 4)))
    w_down = normal_values(key_list[13], (EXPERTS, FF, D), FF ** -0.5, 0.0625, ((1, 4), (2, 8)))
    routes_keys = jax.random.split(jax.random.fold_in(key_list[14], 1), TOKENS // TOKENS)
    routes_turns = jax.random.permutation(jax.random.fold_in(key_list[14], 3), TOKENS // TOKENS)
    routes = jax.vmap(lambda own, number: shared_out(jax.random.fold_in(key_list[14], 2), own, number, TOKENS, EXPERTS, TOPK, CAP, 2))(routes_keys, routes_turns).reshape((TOKENS, TOPK))
    route_logits = normal_values(key_list[15], (TOKENS, TOPK), 1.5, 6.0, (), jnp.float32)
    return {"stream_in": stream_in, "queries": queries, "suffix_keys": suffix_keys, "suffix_values": suffix_values, "prefix_keys": prefix_keys, "prefix_values": prefix_values, "lengths": lengths, "req_group": req_group, "owners": owners, "out_proj": out_proj, "norm_gain": norm_gain, "w_gate": w_gate, "w_up": w_up, "w_down": w_down, "routes": routes, "route_logits": route_logits}


NEGATIVE = -1e+30
EPSILON = 1e-05

def request_tables(lengths, req_group):
    ends = jnp.cumsum(lengths, axis=1)
    places = jnp.arange(TOK_DEV, dtype=jnp.int32)
    local_req = lax.optimization_barrier(jnp.sum((ends[:, None, :] <= places[None, :, None]).astype(jnp.int32), axis=2))
    picks = (local_req[:, :, None] == jnp.arange(REQ_DEV, dtype=jnp.int32)[None, None, :]).astype(jnp.int32)
    group_ids = lax.optimization_barrier(jnp.sum(picks * req_group[:, None, :], axis=2))
    row_base = jnp.arange(N_GX, dtype=jnp.int32)[:, None] * REQ_DEV
    return ((local_req + row_base).reshape(TOKENS), group_ids.reshape(TOKENS))

def reference(stream_in, queries, suffix_keys, suffix_values, prefix_keys, prefix_values, lengths, req_group, owners, out_proj, norm_gain, w_gate, w_up, w_down, routes, route_logits):
    highest = lax.Precision.HIGHEST
    requests, group_ids = request_tables(lengths, req_group)
    per_kv = HEADS // KVH
    scaling = 1.0 / math.sqrt(HD)
    query_blocks = queries.astype(jnp.float32).reshape(TOKENS, KVH, per_kv, HD)
    positions = jnp.arange(TOKENS, dtype=jnp.int32)
    allowed = (requests[:, None] == requests[None, :]) & (positions[None, :] <= positions[:, None])
    suffix_k = suffix_keys.astype(jnp.float32).reshape(TOKENS, KVH, HD)
    suffix_v = suffix_values.astype(jnp.float32).reshape(TOKENS, KVH, HD)
    suffix_scores = jnp.einsum('tcqd,scd->tcqs', query_blocks, suffix_k, precision=highest) * scaling
    score_list = [jnp.where(allowed[:, None, None, :], suffix_scores, NEGATIVE)]
    value_list = [suffix_v]
    for group_id in range(GROUPS):
        holder = owners[group_id]
        slab_keys = lax.dynamic_index_in_dim(prefix_keys, holder, 0, keepdims=False).astype(jnp.float32).reshape(PREFIX, KVH, HD)
        slab_values = lax.dynamic_index_in_dim(prefix_values, holder, 0, keepdims=False).astype(jnp.float32).reshape(PREFIX, KVH, HD)
        group_scores = jnp.einsum('tcqd,pcd->tcqp', query_blocks, slab_keys, precision=highest) * scaling
        score_list.append(jnp.where((group_ids == group_id)[:, None, None, None], group_scores, NEGATIVE))
        value_list.append(slab_values)
    row_max = reduce(jnp.maximum, [lax.optimization_barrier(jnp.max(scores_one, axis=3)) for scores_one in score_list])
    totals = jnp.zeros_like(row_max)
    weighted = jnp.zeros((TOKENS, KVH, per_kv, HD), jnp.float32)
    for scores_one, values_one in zip(score_list, value_list):
        probs = jnp.exp(scores_one - row_max[..., None])
        totals = totals + lax.optimization_barrier(jnp.sum(probs, axis=3))
        weighted = weighted + jnp.einsum('tcqp,pcd->tcqd', probs, values_one, precision=highest)
    attention = (weighted / totals[..., None]).reshape(TOKENS, HEADS * HD).astype(jnp.bfloat16)
    resid = (stream_in.astype(jnp.float32) + jnp.dot(attention, out_proj, preferred_element_type=jnp.float32)).astype(jnp.bfloat16)
    resid_f = resid.astype(jnp.float32)
    scaled = (resid_f * norm_gain.astype(jnp.float32)[None, :]).astype(jnp.bfloat16)
    inverse = 1.0 / jnp.sqrt(lax.optimization_barrier(jnp.sum(resid_f * resid_f, axis=1)) / D + EPSILON)
    route_weights = jax.nn.softmax(route_logits.astype(jnp.float32), axis=1)

    def one_expert(carry, expert):
        gate = jnp.dot(scaled, w_gate[expert], preferred_element_type=jnp.float32) * inverse[:, None]
        upper = jnp.dot(scaled, w_up[expert], preferred_element_type=jnp.float32) * inverse[:, None]
        hidden = (jax.nn.silu(gate) * upper).astype(jnp.bfloat16)
        coeffs = lax.optimization_barrier(jnp.sum(jnp.where(routes == expert, route_weights, 0.0), axis=1))
        output = jnp.dot(hidden, w_down[expert], preferred_element_type=jnp.float32)
        return (carry + coeffs[:, None] * output, None)
    expert_out, unused = lax.scan(one_expert, jnp.zeros((TOKENS, D), jnp.float32), jnp.arange(EXPERTS, dtype=jnp.int32))
    return (resid_f + expert_out).astype(jnp.bfloat16)
```

```python
import math

import jax
import jax.numpy as jnp
from jax import lax
from jax.experimental import pallas as pl
from jax.experimental.pallas import tpu as pltpu
from jax.sharding import PartitionSpec as P

D = 4096
HD = 128
GROUPS = 3
LANES = 128
ROWS = 8
CHUNKS = 2


NEGATIVE = -1e30
EPSILON = 1e-05


def spread(value, axis, source):
    kept = jnp.where(lax.axis_index(axis) == source, value, 0).astype(value.dtype)
    return lax.psum(kept, axis)


def combined_all(value, axis, join):
    pieces = jax.tree.map(lambda part: lax.all_gather(part, axis), value)
    head = jax.tree.map(lambda part: part[0], pieces)
    tail = jax.tree.map(lambda part: part[1:], pieces)
    total, _ = lax.scan(lambda total, section: (join(total, section), None), head, tail)
    return total


def combine_parts(first, second):
    first_max, first_total, first_acc = first
    second_max, second_total, second_acc = second
    joined = jnp.maximum(first_max, second_max)
    first_factor = jnp.exp(first_max - joined)
    second_factor = jnp.exp(second_max - joined)
    return (
        joined,
        first_total * first_factor + second_total * second_factor,
        first_acc * first_factor[..., None] + second_acc * second_factor[..., None],
    )


def body(
    stream_in,
    queries,
    suffix_keys,
    suffix_values,
    prefix_keys,
    prefix_values,
    lengths,
    req_group,
    owners,
    out_proj,
    norm_gain,
    w_gate,
    w_up,
    w_down,
    routes,
    route_logits,
):
    highest = lax.Precision.HIGHEST
    tok_dev = queries.shape[0]
    kv_heads = suffix_keys.shape[1] // HD
    per_kv = queries.shape[1] // suffix_keys.shape[1]
    scaling = 1.0 / math.sqrt(HD)
    gy_index = lax.axis_index("gy")
    places = jnp.arange(tok_dev, dtype=jnp.int32)
    ends = jnp.cumsum(lengths[0])
    requests = jnp.sum((ends[None, :] <= places[:, None]).astype(jnp.int32), axis=1)
    picks = (requests[:, None] == jnp.arange(ends.shape[0], dtype=jnp.int32)[None, :]).astype(
        jnp.int32
    )
    group_ids = jnp.sum(picks * req_group[0][None, :], axis=1)
    query_blocks = queries.reshape(tok_dev, kv_heads, per_kv, HD)
    allowed = (
        (requests[:, None] == requests[None, :])
        & (places[None, :] <= places[:, None])
        & (gy_index == 0)
    )
    suffix_k = suffix_keys.reshape(tok_dev, kv_heads, HD)
    suffix_v = suffix_values.reshape(tok_dev, kv_heads, HD)
    suffix_scores = (
        jnp.einsum("tcqd,scd->tcqs", query_blocks, suffix_k, preferred_element_type=jnp.float32)
        * scaling
    )
    suffix_masked = jnp.where(allowed[:, None, None, :], suffix_scores, NEGATIVE)
    slab_rows = prefix_keys.shape[1]
    score_init = jnp.full((GROUPS, tok_dev, kv_heads, per_kv, slab_rows), NEGATIVE, jnp.float32)
    value_init = jnp.zeros((GROUPS, slab_rows, kv_heads, HD), prefix_values.dtype)

    def one_group(group_id, carry):
        score_stack, value_stack = carry
        holder = lax.dynamic_index_in_dim(owners, group_id, 0, keepdims=False)
        slab_keys, slab_values = (
            spread(prefix_keys[0], "gx", holder),
            spread(prefix_values[0], "gx", holder),
        )
        slab_keys = slab_keys.reshape(-1, kv_heads, HD)
        group_scores = (
            jnp.einsum(
                "tcqd,pcd->tcqp", query_blocks, slab_keys, preferred_element_type=jnp.float32
            )
            * scaling
        )
        masked = jnp.where((group_ids == group_id)[:, None, None, None], group_scores, NEGATIVE)
        score_stack = lax.dynamic_update_index_in_dim(score_stack, masked, group_id, 0)
        value_stack = lax.dynamic_update_index_in_dim(
            value_stack, slab_values.reshape(-1, kv_heads, HD), group_id, 0
        )
        return (score_stack, value_stack)

    score_stack, value_stack = lax.fori_loop(0, GROUPS, one_group, (score_init, value_init))
    prefix_scores = jnp.moveaxis(score_stack, 0, 3).reshape(
        tok_dev, kv_heads, per_kv, GROUPS * slab_rows
    )
    all_scores = jnp.concatenate([suffix_masked, prefix_scores], axis=3)
    all_values = jnp.concatenate(
        [suffix_v, value_stack.reshape(GROUPS * slab_rows, kv_heads, HD)], axis=0
    ).astype(jnp.float32)
    local_max = jnp.max(all_scores, axis=3)
    probs = jnp.exp(all_scores - local_max[..., None])
    local_total = jnp.sum(probs, axis=3)
    local_acc = jnp.einsum("tcqp,pcd->tcqd", probs, all_values, precision=highest)
    merged_max, merged_total, merged_acc = combined_all(
        (local_max, local_total, local_acc), "gy", combine_parts
    )
    attention = (merged_acc / merged_total[..., None]).reshape(tok_dev, -1).astype(jnp.bfloat16)
    resid = (
        stream_in.astype(jnp.float32)
        + jnp.dot(attention, out_proj, preferred_element_type=jnp.float32)
    ).astype(jnp.bfloat16)
    resid_all = lax.all_gather(resid, "gx", axis=0, tiled=True)
    resid_all_f = resid_all.astype(jnp.float32)
    scaled_all = (resid_all_f * norm_gain[None, :]).astype(jnp.bfloat16)
    squares_all = jnp.sum(resid_all_f * resid_all_f, axis=1)
    tokens = resid_all.shape[0]
    experts = w_gate.shape[0]
    width = w_gate.shape[2]
    top_count = routes.shape[1]
    capacity = tokens * 3 // 8
    flat_routes = routes.reshape(-1)
    onehot = (flat_routes[:, None] == jnp.arange(experts, dtype=jnp.int32)[None, :]).astype(
        jnp.int32
    )
    earlier = jnp.cumsum(onehot, axis=0) - onehot
    position = jnp.sum(earlier * onehot, axis=1)
    slot_of_pair = flat_routes * capacity + position
    pair_token = jnp.arange(flat_routes.shape[0], dtype=jnp.int32) // top_count
    matches = slot_of_pair[:, None] == jnp.arange(experts * capacity, dtype=jnp.int32)[None, :]
    slot_token = jnp.sum(jnp.where(matches, pair_token[:, None], 0), axis=0)
    pair_weight = jax.nn.softmax(route_logits, axis=1)
    slot_pairs = slot_of_pair.reshape(tokens, top_count)
    rows_in = jnp.take(scaled_all, slot_token, axis=0).reshape(experts, capacity, -1)
    squares_in = jnp.take(squares_all, slot_token)
    gate_part = jnp.einsum(
        "ecd,edf->ecf", rows_in, w_gate, preferred_element_type=jnp.float32
    ).reshape(experts * capacity, width)
    up_part = jnp.einsum("ecd,edf->ecf", rows_in, w_up, preferred_element_type=jnp.float32).reshape(
        experts * capacity, width
    )
    gate_sum, up_sum, square_sum = lax.psum((gate_part, up_part, squares_in), "gy")
    inverse = 1.0 / jnp.sqrt(square_sum / D + EPSILON)
    hidden = (jax.nn.silu(gate_sum * inverse[:, None]) * (up_sum * inverse[:, None])).astype(
        jnp.bfloat16
    )
    expert_rows = jnp.einsum(
        "ecf,efd->ecd",
        hidden.reshape(experts, capacity, width),
        w_down,
        preferred_element_type=jnp.float32,
    ).reshape(experts * capacity, -1)
    picked = jnp.take(expert_rows, slot_pairs, axis=0)
    expert_out = lax.psum_scatter(
        jnp.sum(picked * pair_weight[..., None], axis=1).astype(jnp.bfloat16),
        "gx",
        scatter_dimension=0,
        tiled=True,
    ).astype(jnp.float32)
    return (resid.astype(jnp.float32) + expert_out).astype(jnp.bfloat16)


def flip(value, axis, size, bit):
    return lax.ppermute(value, axis, [(i, i ^ bit) for i in range(size)])


def attend_kernel(core_ref, q_ref, k_own_ref, v_own_ref, k_far_ref, v_far_ref, out_ref):
    head = pl.program_id(0)
    per_kv = q_ref.shape[1] // HD
    rows = q_ref.shape[0]
    scaling = 1.0 / math.sqrt(HD)
    q = jnp.concatenate([q_ref[:, j * HD : (j + 1) * HD] for j in range(per_kv)], axis=0)
    contract = (((1,), (1,)), ((), ()))
    near = lax.dot_general(q, k_own_ref[0], contract, preferred_element_type=jnp.float32)
    far = lax.dot_general(q, k_far_ref[...], contract, preferred_element_type=jnp.float32)
    top = jnp.maximum(
        jnp.max(near, axis=1, keepdims=True), jnp.max(far, axis=1, keepdims=True)
    )
    factor = scaling * math.log2(math.e)
    near = jnp.exp2((near - top) * factor)
    far = jnp.exp2((far - top) * factor)
    total = jnp.sum(near, axis=1, keepdims=True) + jnp.sum(far, axis=1, keepdims=True)
    acc = jnp.dot(
        near.astype(jnp.bfloat16), v_own_ref[0], preferred_element_type=jnp.float32
    ) + jnp.dot(far.astype(jnp.bfloat16), v_far_ref[...], preferred_element_type=jnp.float32)
    acc = acc / total
    lse = top * scaling + jnp.log(total)
    lanes = lax.broadcasted_iota(jnp.int32, (rows, LANES), 1)
    heads = pl.num_programs(0) * per_kv
    stats = jnp.zeros((rows, LANES), jnp.float32)
    for j in range(per_kv):
        part = lse[j * rows : (j + 1) * rows]
        high = part.astype(jnp.bfloat16).astype(jnp.float32)
        middle = (part - high).astype(jnp.bfloat16).astype(jnp.float32)
        low = part - high - middle
        place = head * per_kv + j
        stats = jnp.where(lanes == place, high, stats)
        stats = jnp.where(lanes == heads + place, middle, stats)
        stats = jnp.where(lanes == 2 * heads + place, low, stats)
        where = pl.multiple_of((head * per_kv + j) * HD, HD)
        out_ref[:, pl.ds(where, HD)] = acc[j * rows : (j + 1) * rows].astype(jnp.bfloat16)
    width = out_ref.shape[1] - LANES

    @pl.when(head == 0)
    def _():
        out_ref[:, width:] = stats.astype(jnp.bfloat16)

    @pl.when(head > 0)
    def _():
        out_ref[:, width:] = (out_ref[:, width:].astype(jnp.float32) + stats).astype(jnp.bfloat16)


def attend(core, q, keys, values, far):
    rows, width = q.shape
    slab = keys.shape[1]
    heads = far.shape[1] // 2 // HD
    span = width // heads
    return pl.pallas_call(
        attend_kernel,
        grid_spec=pltpu.PrefetchScalarGridSpec(
            num_scalar_prefetch=1,
            grid=(heads,),
            in_specs=[
                pl.BlockSpec((rows, span), lambda h, s: (0, h)),
                pl.BlockSpec((1, slab, HD), lambda h, s: (0, 0, s[0] * heads + h)),
                pl.BlockSpec((1, slab, HD), lambda h, s: (0, 0, s[0] * heads + h)),
                pl.BlockSpec((slab, HD), lambda h, s: (0, h)),
                pl.BlockSpec((slab, HD), lambda h, s: (0, heads + h)),
            ],
            out_specs=pl.BlockSpec((rows, width + LANES), lambda h, s: (0, 0)),
        ),
        out_shape=jax.ShapeDtypeStruct((rows, width + LANES), jnp.bfloat16),
        name="attend",
    )(core, q, keys, values, far, far)


def choose_kernel(z_ref, pick_ref, a_ref, b_ref, c_ref, d_ref, *outs):
    pick = pick_ref[...]
    width = a_ref.shape[1] - LANES
    span = outs[0].shape[1] - LANES

    def chosen(where, size):
        first = jnp.where(pick == 1, b_ref[:, where].astype(jnp.float32), a_ref[:, where].astype(jnp.float32))
        second = jnp.where(pick == 3, d_ref[:, where].astype(jnp.float32), c_ref[:, where].astype(jnp.float32))
        return jnp.where(pick >= 2, second, first).astype(jnp.bfloat16)

    stats = chosen(pl.ds(width, LANES), LANES)
    for s, out in enumerate(outs):
        start = pl.multiple_of((z_ref[0] ^ s) * span, LANES)
        out[:, :span] = chosen(pl.ds(start, span), span)
        out[:, span:] = stats


def choose(z, pick, pieces, count):
    rows, width = pieces[0].shape
    span = (width - LANES) // count
    shape = jax.ShapeDtypeStruct((rows, span + LANES), jnp.bfloat16)
    whole = pl.BlockSpec((rows, width), lambda i, s: (0, 0))
    return pl.pallas_call(
        choose_kernel,
        grid_spec=pltpu.PrefetchScalarGridSpec(
            num_scalar_prefetch=1,
            grid=(1,),
            in_specs=[pl.BlockSpec((rows, 1), lambda i, s: (0, 0))] + [whole] * 4,
            out_specs=[pl.BlockSpec((rows, span + LANES), lambda i, s: (0, 0))] * count,
        ),
        out_shape=[shape] * count,
        name="choose",
    )(z, pick, *pieces)


def merge_kernel(place_ref, mask_ref, q_ref, k_ref, v_ref, *refs):
    pieces, out_ref = refs[:-1], refs[-1]
    per_kv = q_ref.shape[1] // HD
    heads = per_kv * len(pieces)
    scaling = 1.0 / math.sqrt(HD)
    allowed = mask_ref[...] > 0
    lanes = lax.broadcasted_iota(jnp.int32, (q_ref.shape[0], LANES), 1)
    stats = [piece[:, per_kv * HD :].astype(jnp.float32) for piece in pieces]
    for j in range(per_kv):
        cols = slice(j * HD, (j + 1) * HD)
        scores = (
            lax.dot_general(
                q_ref[:, cols],
                k_ref[...],
                (((1,), (1,)), ((), ())),
                preferred_element_type=jnp.float32,
            )
            * scaling
        )
        scores = jnp.where(allowed, scores, NEGATIVE)
        top = jnp.max(scores, axis=1, keepdims=True)
        probs = jnp.exp(scores - top)
        base = place_ref[1] * per_kv + j
        mine = (lanes == base) | (lanes == heads + base) | (lanes == 2 * heads + base)
        sizes = [jnp.sum(jnp.where(mine, part, 0.0), axis=1, keepdims=True) for part in stats]
        peak = top
        for size in sizes:
            peak = jnp.maximum(peak, size)
        share = jnp.exp(top - peak)
        total = jnp.sum(probs, axis=1, keepdims=True) * share
        acc = (
            jnp.dot(probs.astype(jnp.bfloat16), v_ref[...], preferred_element_type=jnp.float32)
            * share
        )
        for size, piece in zip(sizes, pieces):
            weight = jnp.exp(size - peak)
            total = total + weight
            acc = acc + weight * piece[:, cols].astype(jnp.float32)
        out_ref[:, cols] = (acc / total).astype(jnp.bfloat16)


def merge(place, mask, queries, suffix_keys, suffix_values, pieces):
    rows = queries.shape[0]
    span = pieces[0].shape[1] - LANES
    piece = pl.BlockSpec((rows, span + LANES), lambda i, s: (0, 0))
    return pl.pallas_call(
        merge_kernel,
        grid_spec=pltpu.PrefetchScalarGridSpec(
            num_scalar_prefetch=1,
            grid=(1,),
            in_specs=[
                pl.BlockSpec((rows, rows), lambda i, s: (0, 0)),
                pl.BlockSpec((rows, span), lambda i, s: (0, s[0])),
                pl.BlockSpec((rows, HD), lambda i, s: (0, s[0])),
                pl.BlockSpec((rows, HD), lambda i, s: (0, s[0])),
            ]
            + [piece] * len(pieces),
            out_specs=pl.BlockSpec((rows, span), lambda i, s: (0, 0)),
        ),
        out_shape=jax.ShapeDtypeStruct((rows, span), jnp.bfloat16),
        name="merge",
    )(place, mask, queries, suffix_keys, suffix_values, *pieces)


def project_kernel(order_ref, stream_ref, weight_ref, *refs):
    pieces, out_ref, acc_ref = refs[:-2], refs[-2], refs[-1]
    step = pl.program_id(0)

    @pl.when(step == 0)
    def _():
        acc_ref[...] = stream_ref[...].astype(jnp.float32)

    for k, piece in enumerate(pieces):

        @pl.when(step == k)
        def _(piece=piece):
            acc_ref[...] += jnp.dot(
                piece[...], weight_ref[...], preferred_element_type=jnp.float32
            )

    @pl.when(step == len(pieces) - 1)
    def _():
        out_ref[...] = acc_ref[...].astype(jnp.bfloat16)


def project(order, stream, weight, pieces):
    rows, width = stream.shape
    span = pieces[0].shape[1]
    return pl.pallas_call(
        project_kernel,
        grid_spec=pltpu.PrefetchScalarGridSpec(
            num_scalar_prefetch=1,
            grid=(len(pieces),),
            in_specs=[
                pl.BlockSpec((rows, width), lambda i, s: (0, 0)),
                pl.BlockSpec((span, width), lambda i, s: (s[i], 0)),
            ]
            + [pl.BlockSpec((rows, span), lambda i, s: (0, 0))] * len(pieces),
            out_specs=pl.BlockSpec((rows, width), lambda i, s: (0, 0)),
            scratch_shapes=[pltpu.VMEM((rows, width), jnp.float32)],
        ),
        out_shape=jax.ShapeDtypeStruct((rows, width), jnp.bfloat16),
        name="project",
    )(order, stream, weight, *pieces)


def widen_kernel(table_ref, rows_ref, gate_ref, up_ref, out_ref, acc_ref):
    expert = pl.program_id(0)
    capacity = rows_ref.shape[1]
    width = gate_ref.shape[2]
    here = pl.ds(pl.multiple_of(table_ref[1 + expert], ROWS), capacity)

    @pl.when(expert == 0)
    def _():
        acc_ref[...] = jnp.zeros(acc_ref.shape, jnp.float32)

    acc_ref[here, :width] = jnp.dot(
        rows_ref[0], gate_ref[0], preferred_element_type=jnp.float32
    )
    acc_ref[here, width:] = jnp.dot(rows_ref[0], up_ref[0], preferred_element_type=jnp.float32)

    @pl.when(expert == pl.num_programs(0) - 1)
    def _():
        out_ref[...] = acc_ref[: out_ref.shape[0], :].astype(jnp.bfloat16)


def widen(table, rows_in, w_gate, w_up, parts, slots):
    experts, capacity, depth = rows_in.shape
    width = w_gate.shape[2] // parts
    weight = pl.BlockSpec((1, depth, width), lambda e, s: (e, 0, s[0]))
    return pl.pallas_call(
        widen_kernel,
        grid_spec=pltpu.PrefetchScalarGridSpec(
            num_scalar_prefetch=1,
            grid=(experts,),
            in_specs=[
                pl.BlockSpec((1, capacity, depth), lambda e, s: (e, 0, 0)),
                weight,
                weight,
            ],
            out_specs=pl.BlockSpec((slots, 2 * width), lambda e, s: (0, 0)),
            scratch_shapes=[pltpu.VMEM((slots + capacity, 2 * width), jnp.float32)],
        ),
        out_shape=jax.ShapeDtypeStruct((slots, 2 * width), jnp.bfloat16),
        name="widen",
    )(table, rows_in, w_gate, w_up)


def narrow_kernel(table_ref, own_ref, far_ref, near_w_ref, far_w_ref, pick_ref, scale_ref, init_ref, out_ref, own_f, far_f):
    expert = pl.program_id(0)
    slots = own_ref.shape[0]
    capacity = pick_ref.shape[1]

    @pl.when(expert == 0)
    def _():
        own_f[:slots, :] = own_ref[...].astype(jnp.float32)
        far_f[:slots, :] = far_ref[...].astype(jnp.float32)
        own_f[slots:, :] = jnp.zeros((capacity, own_f.shape[1]), jnp.float32)
        far_f[slots:, :] = jnp.zeros((capacity, far_f.shape[1]), jnp.float32)
        out_ref[...] = init_ref[...]

    here = pl.ds(pl.multiple_of(table_ref[2 + expert], ROWS), capacity)
    rows = jnp.dot(
        own_f[here, :].astype(jnp.bfloat16), near_w_ref[0], preferred_element_type=jnp.float32
    ) + jnp.dot(
        far_f[here, :].astype(jnp.bfloat16), far_w_ref[0], preferred_element_type=jnp.float32
    )
    rows = (rows * scale_ref[0]).astype(jnp.bfloat16)
    out_ref[...] += lax.dot_general(
        pick_ref[0], rows, (((0,), (0,)), ((), ())), preferred_element_type=jnp.float32
    )


def narrow(table, own, far, w_down, pick, scale, init):
    slots, width = own.shape
    experts, capacity, tokens = pick.shape
    cols = w_down.shape[2]
    return pl.pallas_call(
        narrow_kernel,
        grid_spec=pltpu.PrefetchScalarGridSpec(
            num_scalar_prefetch=1,
            grid=(experts,),
            in_specs=[
                pl.BlockSpec((slots, width), lambda e, s: (0, 0)),
                pl.BlockSpec((slots, width), lambda e, s: (0, 0)),
                pl.BlockSpec((1, width, cols), lambda e, s: (e, s[0], 0)),
                pl.BlockSpec((1, width, cols), lambda e, s: (e, s[1], 0)),
                pl.BlockSpec((1, capacity, tokens), lambda e, s: (e, 0, 0)),
                pl.BlockSpec((1, capacity, 1), lambda e, s: (e, 0, 0)),
                pl.BlockSpec((tokens, cols), lambda e, s: (0, 0)),
            ],
            out_specs=pl.BlockSpec((tokens, cols), lambda e, s: (0, 0)),
            scratch_shapes=[
                pltpu.VMEM((slots + capacity, width), jnp.float32),
                pltpu.VMEM((slots + capacity, width), jnp.float32),
            ],
        ),
        out_shape=jax.ShapeDtypeStruct((tokens, cols), jnp.float32),
        name="narrow",
    )(table, own, far, w_down, w_down, pick, scale, init)


def take_block(value, index, size, axis):
    return lax.dynamic_slice_in_dim(value, index * size, size, axis)


def square_body(
    stream_in,
    queries,
    suffix_keys,
    suffix_values,
    prefix_keys,
    prefix_values,
    lengths,
    req_group,
    owners,
    out_proj,
    norm_gain,
    w_gate,
    w_up,
    w_down,
    routes,
    route_logits,
):
    n_gx, n_gy = 4, 8
    gx_index = lax.axis_index("gx")
    gy_index = lax.axis_index("gy")
    z_index = gy_index // 2
    core = gy_index % 2
    levels = n_gy // 2
    tok_dev = queries.shape[0]
    half_q = queries.shape[1] // 2
    half_kv = prefix_keys.shape[2] // 2
    i32 = jnp.int32
    as_vector = lambda *items: jnp.stack([jnp.asarray(item, i32) for item in items])

    mine_q = take_block(queries, core, half_q, 1)
    far_kv = flip(
        jnp.concatenate(
            [
                take_block(prefix_keys[0], 1 - core, half_kv, 1),
                take_block(prefix_values[0], 1 - core, half_kv, 1),
            ],
            axis=1,
        ),
        "gy",
        n_gy,
        1,
    )
    all_q = [mine_q] + [flip(mine_q, "gx", n_gx, b) for b in range(1, n_gx)]
    core_vec = as_vector(core)
    partial = [attend(core_vec, q, prefix_keys, prefix_values, far_kv) for q in all_q]
    pieces = [partial[0]] + [flip(partial[b], "gx", n_gx, b) for b in range(1, n_gx)]

    places = jnp.arange(tok_dev, dtype=i32)
    lens = lengths[0]
    ends = jnp.sum(
        jnp.where(jnp.arange(lens.shape[0])[:, None] >= jnp.arange(lens.shape[0])[None, :], lens[None, :], 0),
        axis=1,
    )
    requests = jnp.sum((ends[None, :] <= places[:, None]).astype(i32), axis=1)
    holders = jnp.sum(
        jnp.where(req_group[0][:, None] == jnp.arange(GROUPS, dtype=i32)[None, :], owners[None, :], 0),
        axis=1,
    )
    holder = jnp.sum(
        jnp.where(requests[:, None] == jnp.arange(lens.shape[0], dtype=i32)[None, :], holders[None, :], 0),
        axis=1,
    )
    pick = (holder ^ gx_index)[:, None]
    allowed = (
        (requests[:, None] == requests[None, :]) & (places[None, :] <= places[:, None])
    ).astype(jnp.float32)

    chosen = choose(as_vector(z_index), pick, pieces, levels)
    shares = [chosen[0]] + [flip(chosen[s], "gy", n_gy, 2 * s) for s in range(1, levels)]
    block = core * levels + z_index
    heads = merge(
        as_vector(block, z_index), allowed, queries, suffix_keys, suffix_values, shares
    )
    near = [heads] + [flip(heads, "gy", n_gy, 2 * s) for s in range(1, levels)]
    far = flip(jnp.concatenate(near, axis=1), "gy", n_gy, 1)
    span = heads.shape[1]
    features = near + [far[:, s * span : (s + 1) * span] for s in range(levels)]
    order = as_vector(
        *[core * levels + (z_index ^ s) for s in range(levels)],
        *[(1 - core) * levels + (z_index ^ s) for s in range(levels)],
    )
    resid = project(order, stream_in, out_proj, features)

    tokens = n_gx * tok_dev
    experts = w_gate.shape[0]
    capacity = tokens * 3 // 8
    slots = routes.shape[0] * routes.shape[1] + experts * ROWS
    relative = lambda table: jnp.concatenate(
        [take_block(table, gx_index ^ b, tok_dev, 0) for b in range(n_gx)], axis=0
    )
    routes_rel = relative(routes)
    weights_rel = jax.nn.softmax(relative(route_logits), axis=1)
    named = routes_rel[:, :, None] == jnp.arange(experts, dtype=i32)[None, None, :]
    hits = jnp.sum(named.astype(jnp.float32), axis=1)
    weight_of = jnp.sum(jnp.where(named, weights_rel[:, :, None], 0.0), axis=1)
    steps = jnp.arange(tokens, dtype=i32)
    before = (steps[:, None] > steps[None, :]).astype(jnp.bfloat16)
    position = jnp.dot(
        before, hits.astype(jnp.bfloat16), preferred_element_type=jnp.float32
    ).astype(i32)
    counts = jnp.sum(hits, axis=0).astype(i32)
    kinds = jnp.arange(experts, dtype=i32)
    padded = (counts + ROWS - 1) // ROWS * ROWS
    starts = jnp.sum(jnp.where(kinds[:, None] > kinds[None, :], padded[None, :], 0), axis=1)
    place_of = jnp.where(hits > 0, position, -1)
    chosen_row = place_of.T[:, None, :] == jnp.arange(capacity, dtype=i32)[None, :, None]
    row_pick = chosen_row.astype(jnp.bfloat16)
    row_weight = jnp.sum(jnp.where(chosen_row, weight_of.T[:, None, :], 0.0), axis=2)[:, :, None]

    all_resid = jnp.concatenate(
        [resid] + [flip(resid, "gx", n_gx, b) for b in range(1, n_gx)], axis=0
    ).astype(jnp.float32)
    scaled = (all_resid * norm_gain[None, :]).astype(jnp.bfloat16)
    squares = jnp.sum(all_resid * all_resid, axis=1).reshape(-1, LANES)
    for bit in (1, 2, 4):
        squares = squares + flip(squares, "gy", n_gy, bit)
    rstd = 1.0 / jnp.sqrt(squares.reshape(-1) / D + EPSILON)
    rows_in = (
        jnp.dot(
            row_pick.reshape(experts * capacity, tokens),
            scaled,
            preferred_element_type=jnp.float32,
        )
        .astype(jnp.bfloat16)
        .reshape(experts, capacity, -1)
    )

    half_id = (z_index ^ (z_index >> 1)) & 1
    low_id = z_index >> 1
    quarter = half_id * 2 + low_id
    row_ids = quarter * (slots // 4) + jnp.arange(slots // 4, dtype=i32)
    slot_of = jnp.where(hits > 0, starts[None, :] + position, -1)
    owner_mask = jnp.any(row_ids[:, None, None] == slot_of.T[None, :, :], axis=1)
    row_rstd = jnp.sum(jnp.where(owner_mask, rstd[None, :], 0.0), axis=1, keepdims=True)

    f32 = jnp.float32
    parts = 2 * CHUNKS
    rounded = lambda a, b: (a.astype(f32) + b.astype(f32)).astype(jnp.bfloat16)
    sums = []
    for chunk in range(CHUNKS):
        outs = []
        for side in (1 - core, core):
            table = jnp.concatenate([as_vector(2 * chunk + side), starts])
            outs.append(widen(table, rows_in, w_gate, w_up, parts, slots))
        sums.append((outs[1], flip(outs[0], "gy", n_gy, 1)))
    hidden = []
    for keep, seen in sums:
        part = rounded(keep, seen)
        seen = flip(take_block(part, 1 - half_id, slots // 2, 0), "gy", n_gy, 2)
        part = rounded(take_block(part, half_id, slots // 2, 0), seen)
        seen = flip(take_block(part, 1 - low_id, slots // 4, 0), "gy", n_gy, 6)
        part = take_block(part, low_id, slots // 4, 0).astype(f32) + seen.astype(f32)
        width = part.shape[1] // 2
        gate = part[:, :width] * row_rstd
        up = part[:, width:] * row_rstd
        hidden.append((jax.nn.silu(gate) * up).astype(jnp.bfloat16))
    total = jnp.zeros((tokens, w_down.shape[2]), f32)
    for chunk, part in enumerate(hidden):
        seen = flip(part, "gy", n_gy, 6)
        first = low_id == 0
        part = jnp.concatenate([jnp.where(first, part, seen), jnp.where(first, seen, part)], axis=0)
        seen = flip(part, "gy", n_gy, 2)
        first = half_id == 0
        part = jnp.concatenate([jnp.where(first, part, seen), jnp.where(first, seen, part)], axis=0)
        seen = flip(part, "gy", n_gy, 1)
        table = jnp.concatenate([as_vector(2 * chunk + core, 2 * chunk + 1 - core), starts])
        total = narrow(table, part, seen, w_down, row_pick, row_weight, total)
    total = total.astype(jnp.bfloat16)
    back = [total[:tok_dev]] + [
        flip(total[b * tok_dev : (b + 1) * tok_dev], "gx", n_gx, b) for b in range(1, n_gx)
    ]
    expert_out = sum(piece.astype(f32) for piece in back)
    return (resid.astype(f32) + expert_out).astype(jnp.bfloat16)


def fits(mesh, args):
    queries, suffix_keys, prefix_keys = args[1], args[2], args[4]
    return (
        dict(mesh.shape) == {"gx": 4, "gy": 8}
        and suffix_keys.shape[1] == 8 * HD
        and queries.shape[1] % (8 * HD) == 0
        and prefix_keys.shape[2] == 8 * HD
    )


def solution(mesh):
    placed = (
        P("gx", "gy"),
        P("gx", None),
        P("gx", None),
        P("gx", None),
        P("gx", "gy", None),
        P("gx", "gy", None),
        P("gx", None),
        P("gx", None),
        P(),
        P(None, "gy"),
        P("gy"),
        P(None, "gy", "gx"),
        P(None, "gy", "gx"),
        P(None, "gx", "gy"),
        P(),
        P(),
    )

    def run(*args):
        chosen = square_body if fits(mesh, args) else body
        return jax.shard_map(
            chosen, mesh=mesh, in_specs=placed, out_specs=P("gx", "gy"), check_vma=False
        )(*args)

    return run
```

```python
import math

import jax
import jax.numpy as jnp
from jax import lax
from jax.experimental import pallas as pl
from jax.experimental.pallas import tpu as pltpu
from jax.sharding import PartitionSpec as P

D = 4096
HD = 128
GROUPS = 3
LANES = 128
ROWS = 8
PER_STEP = 2
CHUNKS = 2


NEGATIVE = -1e30
EPSILON = 1e-05


def spread(value, axis, source):
    kept = jnp.where(lax.axis_index(axis) == source, value, 0).astype(value.dtype)
    return lax.psum(kept, axis)


def combined_all(value, axis, join):
    pieces = jax.tree.map(lambda part: lax.all_gather(part, axis), value)
    head = jax.tree.map(lambda part: part[0], pieces)
    tail = jax.tree.map(lambda part: part[1:], pieces)
    total, _ = lax.scan(lambda total, section: (join(total, section), None), head, tail)
    return total


def combine_parts(first, second):
    first_max, first_total, first_acc = first
    second_max, second_total, second_acc = second
    joined = jnp.maximum(first_max, second_max)
    first_factor = jnp.exp(first_max - joined)
    second_factor = jnp.exp(second_max - joined)
    return (
        joined,
        first_total * first_factor + second_total * second_factor,
        first_acc * first_factor[..., None] + second_acc * second_factor[..., None],
    )


def body(
    stream_in,
    queries,
    suffix_keys,
    suffix_values,
    prefix_keys,
    prefix_values,
    lengths,
    req_group,
    owners,
    out_proj,
    norm_gain,
    w_gate,
    w_up,
    w_down,
    routes,
    route_logits,
):
    highest = lax.Precision.HIGHEST
    tok_dev = queries.shape[0]
    kv_heads = suffix_keys.shape[1] // HD
    per_kv = queries.shape[1] // suffix_keys.shape[1]
    scaling = 1.0 / math.sqrt(HD)
    gy_index = lax.axis_index("gy")
    places = jnp.arange(tok_dev, dtype=jnp.int32)
    ends = jnp.cumsum(lengths[0])
    requests = jnp.sum((ends[None, :] <= places[:, None]).astype(jnp.int32), axis=1)
    picks = (requests[:, None] == jnp.arange(ends.shape[0], dtype=jnp.int32)[None, :]).astype(
        jnp.int32
    )
    group_ids = jnp.sum(picks * req_group[0][None, :], axis=1)
    query_blocks = queries.reshape(tok_dev, kv_heads, per_kv, HD)
    allowed = (
        (requests[:, None] == requests[None, :])
        & (places[None, :] <= places[:, None])
        & (gy_index == 0)
    )
    suffix_k = suffix_keys.reshape(tok_dev, kv_heads, HD)
    suffix_v = suffix_values.reshape(tok_dev, kv_heads, HD)
    suffix_scores = (
        jnp.einsum("tcqd,scd->tcqs", query_blocks, suffix_k, preferred_element_type=jnp.float32)
        * scaling
    )
    suffix_masked = jnp.where(allowed[:, None, None, :], suffix_scores, NEGATIVE)
    slab_rows = prefix_keys.shape[1]
    score_init = jnp.full((GROUPS, tok_dev, kv_heads, per_kv, slab_rows), NEGATIVE, jnp.float32)
    value_init = jnp.zeros((GROUPS, slab_rows, kv_heads, HD), prefix_values.dtype)

    def one_group(group_id, carry):
        score_stack, value_stack = carry
        holder = lax.dynamic_index_in_dim(owners, group_id, 0, keepdims=False)
        slab_keys, slab_values = (
            spread(prefix_keys[0], "gx", holder),
            spread(prefix_values[0], "gx", holder),
        )
        slab_keys = slab_keys.reshape(-1, kv_heads, HD)
        group_scores = (
            jnp.einsum(
                "tcqd,pcd->tcqp", query_blocks, slab_keys, preferred_element_type=jnp.float32
            )
            * scaling
        )
        masked = jnp.where((group_ids == group_id)[:, None, None, None], group_scores, NEGATIVE)
        score_stack = lax.dynamic_update_index_in_dim(score_stack, masked, group_id, 0)
        value_stack = lax.dynamic_update_index_in_dim(
            value_stack, slab_values.reshape(-1, kv_heads, HD), group_id, 0
        )
        return (score_stack, value_stack)

    score_stack, value_stack = lax.fori_loop(0, GROUPS, one_group, (score_init, value_init))
    prefix_scores = jnp.moveaxis(score_stack, 0, 3).reshape(
        tok_dev, kv_heads, per_kv, GROUPS * slab_rows
    )
    all_scores = jnp.concatenate([suffix_masked, prefix_scores], axis=3)
    all_values = jnp.concatenate(
        [suffix_v, value_stack.reshape(GROUPS * slab_rows, kv_heads, HD)], axis=0
    ).astype(jnp.float32)
    local_max = jnp.max(all_scores, axis=3)
    probs = jnp.exp(all_scores - local_max[..., None])
    local_total = jnp.sum(probs, axis=3)
    local_acc = jnp.einsum("tcqp,pcd->tcqd", probs, all_values, precision=highest)
    merged_max, merged_total, merged_acc = combined_all(
        (local_max, local_total, local_acc), "gy", combine_parts
    )
    attention = (merged_acc / merged_total[..., None]).reshape(tok_dev, -1).astype(jnp.bfloat16)
    resid = (
        stream_in.astype(jnp.float32)
        + jnp.dot(attention, out_proj, preferred_element_type=jnp.float32)
    ).astype(jnp.bfloat16)
    resid_all = lax.all_gather(resid, "gx", axis=0, tiled=True)
    resid_all_f = resid_all.astype(jnp.float32)
    scaled_all = (resid_all_f * norm_gain[None, :]).astype(jnp.bfloat16)
    squares_all = jnp.sum(resid_all_f * resid_all_f, axis=1)
    tokens = resid_all.shape[0]
    experts = w_gate.shape[0]
    width = w_gate.shape[2]
    top_count = routes.shape[1]
    capacity = tokens * 3 // 8
    flat_routes = routes.reshape(-1)
    onehot = (flat_routes[:, None] == jnp.arange(experts, dtype=jnp.int32)[None, :]).astype(
        jnp.int32
    )
    earlier = jnp.cumsum(onehot, axis=0) - onehot
    position = jnp.sum(earlier * onehot, axis=1)
    slot_of_pair = flat_routes * capacity + position
    pair_token = jnp.arange(flat_routes.shape[0], dtype=jnp.int32) // top_count
    matches = slot_of_pair[:, None] == jnp.arange(experts * capacity, dtype=jnp.int32)[None, :]
    slot_token = jnp.sum(jnp.where(matches, pair_token[:, None], 0), axis=0)
    pair_weight = jax.nn.softmax(route_logits, axis=1)
    slot_pairs = slot_of_pair.reshape(tokens, top_count)
    rows_in = jnp.take(scaled_all, slot_token, axis=0).reshape(experts, capacity, -1)
    squares_in = jnp.take(squares_all, slot_token)
    gate_part = jnp.einsum(
        "ecd,edf->ecf", rows_in, w_gate, preferred_element_type=jnp.float32
    ).reshape(experts * capacity, width)
    up_part = jnp.einsum("ecd,edf->ecf", rows_in, w_up, preferred_element_type=jnp.float32).reshape(
        experts * capacity, width
    )
    gate_sum, up_sum, square_sum = lax.psum((gate_part, up_part, squares_in), "gy")
    inverse = 1.0 / jnp.sqrt(square_sum / D + EPSILON)
    hidden = (jax.nn.silu(gate_sum * inverse[:, None]) * (up_sum * inverse[:, None])).astype(
        jnp.bfloat16
    )
    expert_rows = jnp.einsum(
        "ecf,efd->ecd",
        hidden.reshape(experts, capacity, width),
        w_down,
        preferred_element_type=jnp.float32,
    ).reshape(experts * capacity, -1)
    picked = jnp.take(expert_rows, slot_pairs, axis=0)
    expert_out = lax.psum_scatter(
        jnp.sum(picked * pair_weight[..., None], axis=1).astype(jnp.bfloat16),
        "gx",
        scatter_dimension=0,
        tiled=True,
    ).astype(jnp.float32)
    return (resid.astype(jnp.float32) + expert_out).astype(jnp.bfloat16)


def flip(value, axis, size, bit):
    return lax.ppermute(value, axis, [(i, i ^ bit) for i in range(size)])


def attend_kernel(core_ref, q_ref, k_own_ref, v_own_ref, k_far_ref, v_far_ref, out_ref):
    step = pl.program_id(0)
    count = k_far_ref.shape[1] // HD
    per_kv = q_ref.shape[1] // HD // count
    rows = q_ref.shape[0]
    scaling = 1.0 / math.sqrt(HD)
    factor = scaling * math.log2(math.e)
    contract = (((1,), (1,)), ((), ()))
    lanes = lax.broadcasted_iota(jnp.int32, (rows, LANES), 1)
    heads = pl.num_programs(0) * count * per_kv
    stats = jnp.zeros((rows, LANES), jnp.float32)
    for c in range(count):
        cols = slice(c * HD, (c + 1) * HD)
        q = jnp.concatenate(
            [q_ref[:, j * HD : (j + 1) * HD] for j in range(c * per_kv, (c + 1) * per_kv)], axis=0
        )
        near = lax.dot_general(q, k_own_ref[0, :, cols], contract, preferred_element_type=jnp.float32)
        far = lax.dot_general(q, k_far_ref[:, cols], contract, preferred_element_type=jnp.float32)
        top = jnp.maximum(
            jnp.max(near, axis=1, keepdims=True), jnp.max(far, axis=1, keepdims=True)
        )
        near = jnp.exp2((near - top) * factor)
        far = jnp.exp2((far - top) * factor)
        total = jnp.sum(near, axis=1, keepdims=True) + jnp.sum(far, axis=1, keepdims=True)
        acc = jnp.dot(
            near.astype(jnp.bfloat16), v_own_ref[0, :, cols], preferred_element_type=jnp.float32
        ) + jnp.dot(
            far.astype(jnp.bfloat16), v_far_ref[:, cols], preferred_element_type=jnp.float32
        )
        acc = acc / total
        lse = top * scaling + jnp.log(total)
        for j in range(per_kv):
            part = lse[j * rows : (j + 1) * rows]
            high = part.astype(jnp.bfloat16).astype(jnp.float32)
            middle = (part - high).astype(jnp.bfloat16).astype(jnp.float32)
            low = part - high - middle
            place = (step * count + c) * per_kv + j
            stats = jnp.where(lanes == place, high, stats)
            stats = jnp.where(lanes == heads + place, middle, stats)
            stats = jnp.where(lanes == 2 * heads + place, low, stats)
            where = pl.multiple_of(place * HD, HD)
            out_ref[:, pl.ds(where, HD)] = acc[j * rows : (j + 1) * rows].astype(jnp.bfloat16)
    width = out_ref.shape[1] - LANES

    @pl.when(step == 0)
    def _():
        out_ref[:, width:] = stats.astype(jnp.bfloat16)

    @pl.when(step > 0)
    def _():
        out_ref[:, width:] = (out_ref[:, width:].astype(jnp.float32) + stats).astype(jnp.bfloat16)


def attend(core, q, keys, values, far):
    rows, width = q.shape
    slab = keys.shape[1]
    heads = far.shape[1] // 2 // HD
    steps = heads // PER_STEP
    span = width // steps
    depth = PER_STEP * HD
    return pl.pallas_call(
        attend_kernel,
        grid_spec=pltpu.PrefetchScalarGridSpec(
            num_scalar_prefetch=1,
            grid=(steps,),
            in_specs=[
                pl.BlockSpec((rows, span), lambda h, s: (0, h)),
                pl.BlockSpec((1, slab, depth), lambda h, s: (0, 0, s[0] * steps + h)),
                pl.BlockSpec((1, slab, depth), lambda h, s: (0, 0, s[0] * steps + h)),
                pl.BlockSpec((slab, depth), lambda h, s: (0, h)),
                pl.BlockSpec((slab, depth), lambda h, s: (0, steps + h)),
            ],
            out_specs=pl.BlockSpec((rows, width + LANES), lambda h, s: (0, 0)),
        ),
        out_shape=jax.ShapeDtypeStruct((rows, width + LANES), jnp.bfloat16),
        name="attend",
    )(core, q, keys, values, far, far)


def choose_kernel(z_ref, pick_ref, a_ref, b_ref, c_ref, d_ref, *outs):
    pick = pick_ref[...]
    width = a_ref.shape[1] - LANES
    span = outs[0].shape[1] - LANES

    def chosen(where, size):
        first = jnp.where(pick == 1, b_ref[:, where].astype(jnp.float32), a_ref[:, where].astype(jnp.float32))
        second = jnp.where(pick == 3, d_ref[:, where].astype(jnp.float32), c_ref[:, where].astype(jnp.float32))
        return jnp.where(pick >= 2, second, first).astype(jnp.bfloat16)

    stats = chosen(pl.ds(width, LANES), LANES)
    for s, out in enumerate(outs):
        start = pl.multiple_of((z_ref[0] ^ s) * span, LANES)
        out[:, :span] = chosen(pl.ds(start, span), span)
        out[:, span:] = stats


def choose(z, pick, pieces, count):
    rows, width = pieces[0].shape
    span = (width - LANES) // count
    shape = jax.ShapeDtypeStruct((rows, span + LANES), jnp.bfloat16)
    whole = pl.BlockSpec((rows, width), lambda i, s: (0, 0))
    return pl.pallas_call(
        choose_kernel,
        grid_spec=pltpu.PrefetchScalarGridSpec(
            num_scalar_prefetch=1,
            grid=(1,),
            in_specs=[pl.BlockSpec((rows, 1), lambda i, s: (0, 0))] + [whole] * 4,
            out_specs=[pl.BlockSpec((rows, span + LANES), lambda i, s: (0, 0))] * count,
        ),
        out_shape=[shape] * count,
        name="choose",
    )(z, pick, *pieces)


def merge_kernel(place_ref, mask_ref, q_ref, k_ref, v_ref, *refs):
    pieces, out_ref = refs[:-1], refs[-1]
    per_kv = q_ref.shape[1] // HD
    heads = per_kv * len(pieces)
    scaling = 1.0 / math.sqrt(HD)
    allowed = mask_ref[...] > 0
    lanes = lax.broadcasted_iota(jnp.int32, (q_ref.shape[0], LANES), 1)
    stats = [piece[:, per_kv * HD :].astype(jnp.float32) for piece in pieces]
    for j in range(per_kv):
        cols = slice(j * HD, (j + 1) * HD)
        scores = (
            lax.dot_general(
                q_ref[:, cols],
                k_ref[...],
                (((1,), (1,)), ((), ())),
                preferred_element_type=jnp.float32,
            )
            * scaling
        )
        scores = jnp.where(allowed, scores, NEGATIVE)
        top = jnp.max(scores, axis=1, keepdims=True)
        probs = jnp.exp(scores - top)
        base = place_ref[1] * per_kv + j
        mine = (lanes == base) | (lanes == heads + base) | (lanes == 2 * heads + base)
        sizes = [jnp.sum(jnp.where(mine, part, 0.0), axis=1, keepdims=True) for part in stats]
        peak = top
        for size in sizes:
            peak = jnp.maximum(peak, size)
        share = jnp.exp(top - peak)
        total = jnp.sum(probs, axis=1, keepdims=True) * share
        acc = (
            jnp.dot(probs.astype(jnp.bfloat16), v_ref[...], preferred_element_type=jnp.float32)
            * share
        )
        for size, piece in zip(sizes, pieces):
            weight = jnp.exp(size - peak)
            total = total + weight
            acc = acc + weight * piece[:, cols].astype(jnp.float32)
        out_ref[:, cols] = (acc / total).astype(jnp.bfloat16)


def merge(place, mask, queries, suffix_keys, suffix_values, pieces):
    rows = queries.shape[0]
    span = pieces[0].shape[1] - LANES
    piece = pl.BlockSpec((rows, span + LANES), lambda i, s: (0, 0))
    return pl.pallas_call(
        merge_kernel,
        grid_spec=pltpu.PrefetchScalarGridSpec(
            num_scalar_prefetch=1,
            grid=(1,),
            in_specs=[
                pl.BlockSpec((rows, rows), lambda i, s: (0, 0)),
                pl.BlockSpec((rows, span), lambda i, s: (0, s[0])),
                pl.BlockSpec((rows, HD), lambda i, s: (0, s[0])),
                pl.BlockSpec((rows, HD), lambda i, s: (0, s[0])),
            ]
            + [piece] * len(pieces),
            out_specs=pl.BlockSpec((rows, span), lambda i, s: (0, 0)),
        ),
        out_shape=jax.ShapeDtypeStruct((rows, span), jnp.bfloat16),
        name="merge",
    )(place, mask, queries, suffix_keys, suffix_values, *pieces)


def project_kernel(order_ref, stream_ref, *refs):
    count = (len(refs) - 1) // 2
    total = stream_ref[...].astype(jnp.float32)
    for weight, piece in zip(refs[:count], refs[count : 2 * count]):
        total = total + jnp.dot(piece[...], weight[...], preferred_element_type=jnp.float32)
    refs[-1][...] = total.astype(jnp.bfloat16)


def project(order, stream, weight, pieces):
    rows, width = stream.shape
    span = pieces[0].shape[1]
    return pl.pallas_call(
        project_kernel,
        grid_spec=pltpu.PrefetchScalarGridSpec(
            num_scalar_prefetch=1,
            grid=(1,),
            in_specs=[pl.BlockSpec((rows, width), lambda i, s: (0, 0))]
            + [
                pl.BlockSpec((span, width), lambda i, s, k=k: (s[k], 0))
                for k in range(len(pieces))
            ]
            + [pl.BlockSpec((rows, span), lambda i, s: (0, 0))] * len(pieces),
            out_specs=pl.BlockSpec((rows, width), lambda i, s: (0, 0)),
        ),
        out_shape=jax.ShapeDtypeStruct((rows, width), jnp.bfloat16),
        name="project",
    )(order, stream, *[weight] * len(pieces), *pieces)


def widen_kernel(table_ref, rows_ref, gate_ref, up_ref, out_ref, acc_ref):
    step = pl.program_id(0)
    count, capacity = rows_ref.shape[:2]
    width = gate_ref.shape[2]
    filled = out_ref.shape[0] - pl.num_programs(0) * count * ROWS

    @pl.when(step == 0)
    def _():
        acc_ref[filled:, :] = jnp.zeros((acc_ref.shape[0] - filled, 2 * width), jnp.float32)

    for k in range(count):
        here = pl.ds(pl.multiple_of(table_ref[1 + step * count + k], ROWS), capacity)
        acc_ref[here, :width] = jnp.dot(
            rows_ref[k], gate_ref[k], preferred_element_type=jnp.float32
        )
        acc_ref[here, width:] = jnp.dot(
            rows_ref[k], up_ref[k], preferred_element_type=jnp.float32
        )

    @pl.when(step == pl.num_programs(0) - 1)
    def _():
        out_ref[...] = acc_ref[: out_ref.shape[0], :].astype(jnp.bfloat16)


def widen(table, rows_in, w_gate, w_up, parts, slots):
    experts, capacity, depth = rows_in.shape
    width = w_gate.shape[2] // parts
    weight = pl.BlockSpec((PER_STEP, depth, width), lambda e, s: (e, 0, s[0]))
    return pl.pallas_call(
        widen_kernel,
        grid_spec=pltpu.PrefetchScalarGridSpec(
            num_scalar_prefetch=1,
            grid=(experts // PER_STEP,),
            in_specs=[
                pl.BlockSpec((PER_STEP, capacity, depth), lambda e, s: (e, 0, 0)),
                weight,
                weight,
            ],
            out_specs=pl.BlockSpec((slots, 2 * width), lambda e, s: (0, 0)),
            scratch_shapes=[pltpu.VMEM((slots + capacity, 2 * width), jnp.float32)],
        ),
        out_shape=jax.ShapeDtypeStruct((slots, 2 * width), jnp.bfloat16),
        name="widen",
    )(table, rows_in, w_gate, w_up)


def narrow_kernel(table_ref, own_ref, far_ref, near_w_ref, far_w_ref, pick_ref, scale_ref, init_ref, out_ref, own_f, far_f):
    step = pl.program_id(0)
    slots = own_ref.shape[0]
    count, capacity = pick_ref.shape[:2]

    @pl.when(step == 0)
    def _():
        own_f[:slots, :] = own_ref[...].astype(jnp.float32)
        far_f[:slots, :] = far_ref[...].astype(jnp.float32)
        own_f[slots:, :] = jnp.zeros((capacity, own_f.shape[1]), jnp.float32)
        far_f[slots:, :] = jnp.zeros((capacity, far_f.shape[1]), jnp.float32)
        out_ref[...] = init_ref[...]

    for k in range(count):
        here = pl.ds(pl.multiple_of(table_ref[2 + step * count + k], ROWS), capacity)
        rows = jnp.dot(
            own_f[here, :].astype(jnp.bfloat16), near_w_ref[k], preferred_element_type=jnp.float32
        ) + jnp.dot(
            far_f[here, :].astype(jnp.bfloat16), far_w_ref[k], preferred_element_type=jnp.float32
        )
        rows = (rows * scale_ref[k]).astype(jnp.bfloat16)
        out_ref[...] += lax.dot_general(
            pick_ref[k], rows, (((0,), (0,)), ((), ())), preferred_element_type=jnp.float32
        )


def narrow(table, own, far, w_down, pick, scale, init):
    slots, width = own.shape
    experts, capacity, tokens = pick.shape
    cols = w_down.shape[2]
    return pl.pallas_call(
        narrow_kernel,
        grid_spec=pltpu.PrefetchScalarGridSpec(
            num_scalar_prefetch=1,
            grid=(experts // PER_STEP,),
            in_specs=[
                pl.BlockSpec((slots, width), lambda e, s: (0, 0)),
                pl.BlockSpec((slots, width), lambda e, s: (0, 0)),
                pl.BlockSpec((PER_STEP, width, cols), lambda e, s: (e, s[0], 0)),
                pl.BlockSpec((PER_STEP, width, cols), lambda e, s: (e, s[1], 0)),
                pl.BlockSpec((PER_STEP, capacity, tokens), lambda e, s: (e, 0, 0)),
                pl.BlockSpec((PER_STEP, capacity, 1), lambda e, s: (e, 0, 0)),
                pl.BlockSpec((tokens, cols), lambda e, s: (0, 0)),
            ],
            out_specs=pl.BlockSpec((tokens, cols), lambda e, s: (0, 0)),
            scratch_shapes=[
                pltpu.VMEM((slots + capacity, width), jnp.float32),
                pltpu.VMEM((slots + capacity, width), jnp.float32),
            ],
        ),
        out_shape=jax.ShapeDtypeStruct((tokens, cols), jnp.float32),
        name="narrow",
    )(table, own, far, w_down, w_down, pick, scale, init)


def take_block(value, index, size, axis):
    return lax.dynamic_slice_in_dim(value, index * size, size, axis)


def square_body(
    stream_in,
    queries,
    suffix_keys,
    suffix_values,
    prefix_keys,
    prefix_values,
    lengths,
    req_group,
    owners,
    out_proj,
    norm_gain,
    w_gate,
    w_up,
    w_down,
    routes,
    route_logits,
):
    n_gx, n_gy = 4, 8
    gx_index = lax.axis_index("gx")
    gy_index = lax.axis_index("gy")
    z_index = gy_index // 2
    core = gy_index % 2
    levels = n_gy // 2
    tok_dev = queries.shape[0]
    half_q = queries.shape[1] // 2
    half_kv = prefix_keys.shape[2] // 2
    i32 = jnp.int32
    as_vector = lambda *items: jnp.stack([jnp.asarray(item, i32) for item in items])

    mine_q = take_block(queries, core, half_q, 1)
    far_kv = flip(
        jnp.concatenate(
            [
                take_block(prefix_keys[0], 1 - core, half_kv, 1),
                take_block(prefix_values[0], 1 - core, half_kv, 1),
            ],
            axis=1,
        ),
        "gy",
        n_gy,
        1,
    )
    all_q = [mine_q] + [flip(mine_q, "gx", n_gx, b) for b in range(1, n_gx)]
    core_vec = as_vector(core)
    partial = [attend(core_vec, q, prefix_keys, prefix_values, far_kv) for q in all_q]
    pieces = [partial[0]] + [flip(partial[b], "gx", n_gx, b) for b in range(1, n_gx)]

    places = jnp.arange(tok_dev, dtype=i32)
    lens = lengths[0]
    ends = jnp.sum(
        jnp.where(jnp.arange(lens.shape[0])[:, None] >= jnp.arange(lens.shape[0])[None, :], lens[None, :], 0),
        axis=1,
    )
    requests = jnp.sum((ends[None, :] <= places[:, None]).astype(i32), axis=1)
    holders = jnp.sum(
        jnp.where(req_group[0][:, None] == jnp.arange(GROUPS, dtype=i32)[None, :], owners[None, :], 0),
        axis=1,
    )
    holder = jnp.sum(
        jnp.where(requests[:, None] == jnp.arange(lens.shape[0], dtype=i32)[None, :], holders[None, :], 0),
        axis=1,
    )
    pick = (holder ^ gx_index)[:, None]
    allowed = (
        (requests[:, None] == requests[None, :]) & (places[None, :] <= places[:, None])
    ).astype(jnp.float32)

    chosen = choose(as_vector(z_index), pick, pieces, levels)
    shares = [chosen[0]] + [flip(chosen[s], "gy", n_gy, 2 * s) for s in range(1, levels)]
    block = core * levels + z_index
    heads = merge(
        as_vector(block, z_index), allowed, queries, suffix_keys, suffix_values, shares
    )
    near = [heads] + [flip(heads, "gy", n_gy, 2 * s) for s in range(1, levels)]
    far = flip(jnp.concatenate(near, axis=1), "gy", n_gy, 1)
    span = heads.shape[1]
    features = near + [far[:, s * span : (s + 1) * span] for s in range(levels)]
    order = as_vector(
        *[core * levels + (z_index ^ s) for s in range(levels)],
        *[(1 - core) * levels + (z_index ^ s) for s in range(levels)],
    )
    resid = project(order, stream_in, out_proj, features)

    tokens = n_gx * tok_dev
    experts = w_gate.shape[0]
    capacity = tokens * 3 // 8
    slots = routes.shape[0] * routes.shape[1] + experts * ROWS
    relative = lambda table: jnp.concatenate(
        [take_block(table, gx_index ^ b, tok_dev, 0) for b in range(n_gx)], axis=0
    )
    routes_rel = relative(routes)
    weights_rel = jax.nn.softmax(relative(route_logits), axis=1)
    named = routes_rel[:, :, None] == jnp.arange(experts, dtype=i32)[None, None, :]
    hits = jnp.sum(named.astype(jnp.float32), axis=1)
    weight_of = jnp.sum(jnp.where(named, weights_rel[:, :, None], 0.0), axis=1)
    steps = jnp.arange(tokens, dtype=i32)
    before = (steps[:, None] > steps[None, :]).astype(jnp.bfloat16)
    position = jnp.dot(
        before, hits.astype(jnp.bfloat16), preferred_element_type=jnp.float32
    ).astype(i32)
    counts = jnp.sum(hits, axis=0).astype(i32)
    kinds = jnp.arange(experts, dtype=i32)
    padded = (counts + ROWS - 1) // ROWS * ROWS
    starts = jnp.sum(jnp.where(kinds[:, None] > kinds[None, :], padded[None, :], 0), axis=1)
    place_of = jnp.where(hits > 0, position, -1)
    chosen_row = place_of.T[:, None, :] == jnp.arange(capacity, dtype=i32)[None, :, None]
    row_pick = chosen_row.astype(jnp.bfloat16)
    row_weight = jnp.sum(jnp.where(chosen_row, weight_of.T[:, None, :], 0.0), axis=2)[:, :, None]

    all_resid = jnp.concatenate(
        [resid] + [flip(resid, "gx", n_gx, b) for b in range(1, n_gx)], axis=0
    ).astype(jnp.float32)
    scaled = (all_resid * norm_gain[None, :]).astype(jnp.bfloat16)
    squares = jnp.sum(all_resid * all_resid, axis=1).reshape(-1, LANES)
    rows_in = (
        jnp.dot(
            row_pick.reshape(experts * capacity, tokens),
            scaled,
            preferred_element_type=jnp.float32,
        )
        .astype(jnp.bfloat16)
        .reshape(experts, capacity, -1)
    )

    near_id = (z_index ^ (z_index >> 1)) & 1
    wrap_id = z_index >> 1
    routes_z = [((near_id, 2), (wrap_id, 6)), ((wrap_id, 6), (near_id, 2))]
    slot_of = jnp.where(hits > 0, starts[None, :] + position, -1)

    def quarter_rstd(quarter):
        row_ids = quarter * (slots // 4) + jnp.arange(slots // 4, dtype=i32)
        owner_mask = jnp.any(row_ids[:, None, None] == slot_of.T[None, :, :], axis=1)
        return jnp.sum(jnp.where(owner_mask, rstd[None, :], 0.0), axis=1, keepdims=True)

    f32 = jnp.float32
    parts = 2 * CHUNKS
    rounded = lambda a, b: (a.astype(f32) + b.astype(f32)).astype(jnp.bfloat16)
    halves = []
    for chunk in range(CHUNKS):
        (half_id, half_bit), _ = routes_z[chunk % 2]
        tables = [
            jnp.concatenate([as_vector(2 * chunk + side), starts]) for side in (1 - core, core)
        ]
        away = widen(tables[0], rows_in, w_gate, w_up, parts, slots)
        rows_in, away = lax.optimization_barrier((rows_in, away))
        seen = flip(away, "gy", n_gy, 1)
        keep = widen(tables[1], rows_in, w_gate, w_up, parts, slots)
        part = rounded(keep, seen)
        send = take_block(part, 1 - half_id, slots // 2, 0)
        keep = take_block(part, half_id, slots // 2, 0)
        rows_in, send, keep, squares = lax.optimization_barrier((rows_in, send, keep, squares))
        halves.append((keep, flip(send, "gy", n_gy, half_bit)))
    for bit in (1, 2, 4):
        squares = squares + flip(squares, "gy", n_gy, bit)
    rstd = 1.0 / jnp.sqrt(squares.reshape(-1) / D + EPSILON)
    hidden = []
    for chunk, (keep, seen) in enumerate(halves):
        (half_id, _), (low_id, low_bit) = routes_z[chunk % 2]
        part = rounded(keep, seen)
        seen = flip(take_block(part, 1 - low_id, slots // 4, 0), "gy", n_gy, low_bit)
        part = take_block(part, low_id, slots // 4, 0).astype(f32) + seen.astype(f32)
        width = part.shape[1] // 2
        row_rstd = quarter_rstd(half_id * 2 + low_id)
        gate = part[:, :width] * row_rstd
        up = part[:, width:] * row_rstd
        hidden.append((jax.nn.silu(gate) * up).astype(jnp.bfloat16))
    total = jnp.zeros((tokens, w_down.shape[2]), f32)
    for chunk, part in enumerate(hidden):
        for index, bit in routes_z[chunk % 2][::-1]:
            seen = flip(part, "gy", n_gy, bit)
            first = index == 0
            part = jnp.concatenate(
                [jnp.where(first, part, seen), jnp.where(first, seen, part)], axis=0
            )
        seen = flip(part, "gy", n_gy, 1)
        table = jnp.concatenate([as_vector(2 * chunk + core, 2 * chunk + 1 - core), starts])
        total = narrow(table, part, seen, w_down, row_pick, row_weight, total)
    total = total.astype(jnp.bfloat16)
    back = [total[:tok_dev]] + [
        flip(total[b * tok_dev : (b + 1) * tok_dev], "gx", n_gx, b) for b in range(1, n_gx)
    ]
    expert_out = sum(piece.astype(f32) for piece in back)
    return (resid.astype(f32) + expert_out).astype(jnp.bfloat16)


def fits(mesh, args):
    queries, suffix_keys, prefix_keys = args[1], args[2], args[4]
    return (
        dict(mesh.shape) == {"gx": 4, "gy": 8}
        and suffix_keys.shape[1] == 8 * HD
        and queries.shape[1] % (8 * HD) == 0
        and prefix_keys.shape[2] == 8 * HD
    )


def solution(mesh):
    placed = (
        P("gx", "gy"),
        P("gx", None),
        P("gx", None),
        P("gx", None),
        P("gx", "gy", None),
        P("gx", "gy", None),
        P("gx", None),
        P("gx", None),
        P(),
        P(None, "gy"),
        P("gy"),
        P(None, "gy", "gx"),
        P(None, "gy", "gx"),
        P(None, "gx", "gy"),
        P(),
        P(),
    )

    def run(*args):
        chosen = square_body if fits(mesh, args) else body
        return jax.shard_map(
            chosen, mesh=mesh, in_specs=placed, out_specs=P("gx", "gy"), check_vma=False
        )(*args)

    return run
```

```python
import math

import jax
import jax.numpy as jnp
from jax import lax
from jax.experimental import pallas as pl
from jax.experimental.pallas import tpu as pltpu
from jax.sharding import PartitionSpec as P

D = 4096
HD = 128
GROUPS = 3
LANES = 128
ROWS = 8
PER_STEP = 2
CHUNKS = 2


NEGATIVE = -1e30
EPSILON = 1e-05


def spread(value, axis, source):
    kept = jnp.where(lax.axis_index(axis) == source, value, 0).astype(value.dtype)
    return lax.psum(kept, axis)


def combined_all(value, axis, join):
    pieces = jax.tree.map(lambda part: lax.all_gather(part, axis), value)
    head = jax.tree.map(lambda part: part[0], pieces)
    tail = jax.tree.map(lambda part: part[1:], pieces)
    total, _ = lax.scan(lambda total, section: (join(total, section), None), head, tail)
    return total


def combine_parts(first, second):
    first_max, first_total, first_acc = first
    second_max, second_total, second_acc = second
    joined = jnp.maximum(first_max, second_max)
    first_factor = jnp.exp(first_max - joined)
    second_factor = jnp.exp(second_max - joined)
    return (
        joined,
        first_total * first_factor + second_total * second_factor,
        first_acc * first_factor[..., None] + second_acc * second_factor[..., None],
    )


def body(
    stream_in,
    queries,
    suffix_keys,
    suffix_values,
    prefix_keys,
    prefix_values,
    lengths,
    req_group,
    owners,
    out_proj,
    norm_gain,
    w_gate,
    w_up,
    w_down,
    routes,
    route_logits,
):
    highest = lax.Precision.HIGHEST
    tok_dev = queries.shape[0]
    kv_heads = suffix_keys.shape[1] // HD
    per_kv = queries.shape[1] // suffix_keys.shape[1]
    scaling = 1.0 / math.sqrt(HD)
    gy_index = lax.axis_index("gy")
    places = jnp.arange(tok_dev, dtype=jnp.int32)
    ends = jnp.cumsum(lengths[0])
    requests = jnp.sum((ends[None, :] <= places[:, None]).astype(jnp.int32), axis=1)
    picks = (requests[:, None] == jnp.arange(ends.shape[0], dtype=jnp.int32)[None, :]).astype(
        jnp.int32
    )
    group_ids = jnp.sum(picks * req_group[0][None, :], axis=1)
    query_blocks = queries.reshape(tok_dev, kv_heads, per_kv, HD)
    allowed = (
        (requests[:, None] == requests[None, :])
        & (places[None, :] <= places[:, None])
        & (gy_index == 0)
    )
    suffix_k = suffix_keys.reshape(tok_dev, kv_heads, HD)
    suffix_v = suffix_values.reshape(tok_dev, kv_heads, HD)
    suffix_scores = (
        jnp.einsum("tcqd,scd->tcqs", query_blocks, suffix_k, preferred_element_type=jnp.float32)
        * scaling
    )
    suffix_masked = jnp.where(allowed[:, None, None, :], suffix_scores, NEGATIVE)
    slab_rows = prefix_keys.shape[1]
    score_init = jnp.full((GROUPS, tok_dev, kv_heads, per_kv, slab_rows), NEGATIVE, jnp.float32)
    value_init = jnp.zeros((GROUPS, slab_rows, kv_heads, HD), prefix_values.dtype)

    def one_group(group_id, carry):
        score_stack, value_stack = carry
        holder = lax.dynamic_index_in_dim(owners, group_id, 0, keepdims=False)
        slab_keys, slab_values = (
            spread(prefix_keys[0], "gx", holder),
            spread(prefix_values[0], "gx", holder),
        )
        slab_keys = slab_keys.reshape(-1, kv_heads, HD)
        group_scores = (
            jnp.einsum(
                "tcqd,pcd->tcqp", query_blocks, slab_keys, preferred_element_type=jnp.float32
            )
            * scaling
        )
        masked = jnp.where((group_ids == group_id)[:, None, None, None], group_scores, NEGATIVE)
        score_stack = lax.dynamic_update_index_in_dim(score_stack, masked, group_id, 0)
        value_stack = lax.dynamic_update_index_in_dim(
            value_stack, slab_values.reshape(-1, kv_heads, HD), group_id, 0
        )
        return (score_stack, value_stack)

    score_stack, value_stack = lax.fori_loop(0, GROUPS, one_group, (score_init, value_init))
    prefix_scores = jnp.moveaxis(score_stack, 0, 3).reshape(
        tok_dev, kv_heads, per_kv, GROUPS * slab_rows
    )
    all_scores = jnp.concatenate([suffix_masked, prefix_scores], axis=3)
    all_values = jnp.concatenate(
        [suffix_v, value_stack.reshape(GROUPS * slab_rows, kv_heads, HD)], axis=0
    ).astype(jnp.float32)
    local_max = jnp.max(all_scores, axis=3)
    probs = jnp.exp(all_scores - local_max[..., None])
    local_total = jnp.sum(probs, axis=3)
    local_acc = jnp.einsum("tcqp,pcd->tcqd", probs, all_values, precision=highest)
    merged_max, merged_total, merged_acc = combined_all(
        (local_max, local_total, local_acc), "gy", combine_parts
    )
    attention = (merged_acc / merged_total[..., None]).reshape(tok_dev, -1).astype(jnp.bfloat16)
    resid = (
        stream_in.astype(jnp.float32)
        + jnp.dot(attention, out_proj, preferred_element_type=jnp.float32)
    ).astype(jnp.bfloat16)
    resid_all = lax.all_gather(resid, "gx", axis=0, tiled=True)
    resid_all_f = resid_all.astype(jnp.float32)
    scaled_all = (resid_all_f * norm_gain[None, :]).astype(jnp.bfloat16)
    squares_all = jnp.sum(resid_all_f * resid_all_f, axis=1)
    tokens = resid_all.shape[0]
    experts = w_gate.shape[0]
    width = w_gate.shape[2]
    top_count = routes.shape[1]
    capacity = tokens * 3 // 8
    flat_routes = routes.reshape(-1)
    onehot = (flat_routes[:, None] == jnp.arange(experts, dtype=jnp.int32)[None, :]).astype(
        jnp.int32
    )
    earlier = jnp.cumsum(onehot, axis=0) - onehot
    position = jnp.sum(earlier * onehot, axis=1)
    slot_of_pair = flat_routes * capacity + position
    pair_token = jnp.arange(flat_routes.shape[0], dtype=jnp.int32) // top_count
    matches = slot_of_pair[:, None] == jnp.arange(experts * capacity, dtype=jnp.int32)[None, :]
    slot_token = jnp.sum(jnp.where(matches, pair_token[:, None], 0), axis=0)
    pair_weight = jax.nn.softmax(route_logits, axis=1)
    slot_pairs = slot_of_pair.reshape(tokens, top_count)
    rows_in = jnp.take(scaled_all, slot_token, axis=0).reshape(experts, capacity, -1)
    squares_in = jnp.take(squares_all, slot_token)
    gate_part = jnp.einsum(
        "ecd,edf->ecf", rows_in, w_gate, preferred_element_type=jnp.float32
    ).reshape(experts * capacity, width)
    up_part = jnp.einsum("ecd,edf->ecf", rows_in, w_up, preferred_element_type=jnp.float32).reshape(
        experts * capacity, width
    )
    gate_sum, up_sum, square_sum = lax.psum((gate_part, up_part, squares_in), "gy")
    inverse = 1.0 / jnp.sqrt(square_sum / D + EPSILON)
    hidden = (jax.nn.silu(gate_sum * inverse[:, None]) * (up_sum * inverse[:, None])).astype(
        jnp.bfloat16
    )
    expert_rows = jnp.einsum(
        "ecf,efd->ecd",
        hidden.reshape(experts, capacity, width),
        w_down,
        preferred_element_type=jnp.float32,
    ).reshape(experts * capacity, -1)
    picked = jnp.take(expert_rows, slot_pairs, axis=0)
    expert_out = lax.psum_scatter(
        jnp.sum(picked * pair_weight[..., None], axis=1).astype(jnp.bfloat16),
        "gx",
        scatter_dimension=0,
        tiled=True,
    ).astype(jnp.float32)
    return (resid.astype(jnp.float32) + expert_out).astype(jnp.bfloat16)


def flip(value, axis, size, bit):
    return lax.ppermute(value, axis, [(i, i ^ bit) for i in range(size)])


def attend_kernel(core_ref, q_ref, k_own_ref, v_own_ref, k_far_ref, v_far_ref, out_ref):
    step = pl.program_id(0)
    count = k_far_ref.shape[1] // HD
    per_kv = q_ref.shape[1] // HD // count
    rows = q_ref.shape[0]
    scaling = 1.0 / math.sqrt(HD)
    factor = scaling * math.log2(math.e)
    contract = (((1,), (1,)), ((), ()))
    lanes = lax.broadcasted_iota(jnp.int32, (rows, LANES), 1)
    heads = pl.num_programs(0) * count * per_kv
    stats = jnp.zeros((rows, LANES), jnp.float32)
    for c in range(count):
        cols = slice(c * HD, (c + 1) * HD)
        q = jnp.concatenate(
            [q_ref[:, j * HD : (j + 1) * HD] for j in range(c * per_kv, (c + 1) * per_kv)], axis=0
        )
        near = lax.dot_general(q, k_own_ref[0, :, cols], contract, preferred_element_type=jnp.float32)
        far = lax.dot_general(q, k_far_ref[:, cols], contract, preferred_element_type=jnp.float32)
        top = jnp.maximum(
            jnp.max(near, axis=1, keepdims=True), jnp.max(far, axis=1, keepdims=True)
        )
        near = jnp.exp2((near - top) * factor)
        far = jnp.exp2((far - top) * factor)
        total = jnp.sum(near, axis=1, keepdims=True) + jnp.sum(far, axis=1, keepdims=True)
        acc = jnp.dot(
            near.astype(jnp.bfloat16), v_own_ref[0, :, cols], preferred_element_type=jnp.float32
        ) + jnp.dot(
            far.astype(jnp.bfloat16), v_far_ref[:, cols], preferred_element_type=jnp.float32
        )
        acc = acc / total
        lse = top * scaling + jnp.log(total)
        for j in range(per_kv):
            part = lse[j * rows : (j + 1) * rows]
            high = part.astype(jnp.bfloat16).astype(jnp.float32)
            middle = (part - high).astype(jnp.bfloat16).astype(jnp.float32)
            low = part - high - middle
            place = (step * count + c) * per_kv + j
            stats = jnp.where(lanes == place, high, stats)
            stats = jnp.where(lanes == heads + place, middle, stats)
            stats = jnp.where(lanes == 2 * heads + place, low, stats)
            where = pl.multiple_of(place * HD, HD)
            out_ref[:, pl.ds(where, HD)] = acc[j * rows : (j + 1) * rows].astype(jnp.bfloat16)
    width = out_ref.shape[1] - LANES

    @pl.when(step == 0)
    def _():
        out_ref[:, width:] = stats.astype(jnp.bfloat16)

    @pl.when(step > 0)
    def _():
        out_ref[:, width:] = (out_ref[:, width:].astype(jnp.float32) + stats).astype(jnp.bfloat16)


def attend(core, q, keys, values, far):
    rows, width = q.shape
    slab = keys.shape[1]
    heads = far.shape[1] // 2 // HD
    steps = heads // PER_STEP
    span = width // steps
    depth = PER_STEP * HD
    return pl.pallas_call(
        attend_kernel,
        grid_spec=pltpu.PrefetchScalarGridSpec(
            num_scalar_prefetch=1,
            grid=(steps,),
            in_specs=[
                pl.BlockSpec((rows, span), lambda h, s: (0, h)),
                pl.BlockSpec((1, slab, depth), lambda h, s: (0, 0, s[0] * steps + h)),
                pl.BlockSpec((1, slab, depth), lambda h, s: (0, 0, s[0] * steps + h)),
                pl.BlockSpec((slab, depth), lambda h, s: (0, h)),
                pl.BlockSpec((slab, depth), lambda h, s: (0, steps + h)),
            ],
            out_specs=pl.BlockSpec((rows, width + LANES), lambda h, s: (0, 0)),
        ),
        out_shape=jax.ShapeDtypeStruct((rows, width + LANES), jnp.bfloat16),
        name="attend",
    )(core, q, keys, values, far, far)


def choose_kernel(z_ref, pick_ref, a_ref, b_ref, c_ref, d_ref, *outs):
    pick = pick_ref[...]
    width = a_ref.shape[1] - LANES
    span = outs[0].shape[1] - LANES

    def chosen(where, size):
        first = jnp.where(pick == 1, b_ref[:, where].astype(jnp.float32), a_ref[:, where].astype(jnp.float32))
        second = jnp.where(pick == 3, d_ref[:, where].astype(jnp.float32), c_ref[:, where].astype(jnp.float32))
        return jnp.where(pick >= 2, second, first).astype(jnp.bfloat16)

    stats = chosen(pl.ds(width, LANES), LANES)
    for s, out in enumerate(outs):
        start = pl.multiple_of((z_ref[0] ^ s) * span, LANES)
        out[:, :span] = chosen(pl.ds(start, span), span)
        out[:, span:] = stats


def choose(z, pick, pieces, count):
    rows, width = pieces[0].shape
    span = (width - LANES) // count
    shape = jax.ShapeDtypeStruct((rows, span + LANES), jnp.bfloat16)
    whole = pl.BlockSpec((rows, width), lambda i, s: (0, 0))
    return pl.pallas_call(
        choose_kernel,
        grid_spec=pltpu.PrefetchScalarGridSpec(
            num_scalar_prefetch=1,
            grid=(1,),
            in_specs=[pl.BlockSpec((rows, 1), lambda i, s: (0, 0))] + [whole] * 4,
            out_specs=[pl.BlockSpec((rows, span + LANES), lambda i, s: (0, 0))] * count,
        ),
        out_shape=[shape] * count,
        name="choose",
    )(z, pick, *pieces)


def merge_kernel(place_ref, mask_ref, q_ref, k_ref, v_ref, *refs):
    pieces, out_ref = refs[:-1], refs[-1]
    per_kv = q_ref.shape[1] // HD
    heads = per_kv * len(pieces)
    scaling = 1.0 / math.sqrt(HD)
    allowed = mask_ref[...] > 0
    lanes = lax.broadcasted_iota(jnp.int32, (q_ref.shape[0], LANES), 1)
    stats = [piece[:, per_kv * HD :].astype(jnp.float32) for piece in pieces]
    for j in range(per_kv):
        cols = slice(j * HD, (j + 1) * HD)
        scores = (
            lax.dot_general(
                q_ref[:, cols],
                k_ref[...],
                (((1,), (1,)), ((), ())),
                preferred_element_type=jnp.float32,
            )
            * scaling
        )
        scores = jnp.where(allowed, scores, NEGATIVE)
        top = jnp.max(scores, axis=1, keepdims=True)
        probs = jnp.exp(scores - top)
        base = place_ref[1] * per_kv + j
        mine = (lanes == base) | (lanes == heads + base) | (lanes == 2 * heads + base)
        sizes = [jnp.sum(jnp.where(mine, part, 0.0), axis=1, keepdims=True) for part in stats]
        peak = top
        for size in sizes:
            peak = jnp.maximum(peak, size)
        share = jnp.exp(top - peak)
        total = jnp.sum(probs, axis=1, keepdims=True) * share
        acc = (
            jnp.dot(probs.astype(jnp.bfloat16), v_ref[...], preferred_element_type=jnp.float32)
            * share
        )
        for size, piece in zip(sizes, pieces):
            weight = jnp.exp(size - peak)
            total = total + weight
            acc = acc + weight * piece[:, cols].astype(jnp.float32)
        out_ref[:, cols] = (acc / total).astype(jnp.bfloat16)


def merge(place, mask, queries, suffix_keys, suffix_values, pieces):
    rows = queries.shape[0]
    span = pieces[0].shape[1] - LANES
    piece = pl.BlockSpec((rows, span + LANES), lambda i, s: (0, 0))
    return pl.pallas_call(
        merge_kernel,
        grid_spec=pltpu.PrefetchScalarGridSpec(
            num_scalar_prefetch=1,
            grid=(1,),
            in_specs=[
                pl.BlockSpec((rows, rows), lambda i, s: (0, 0)),
                pl.BlockSpec((rows, span), lambda i, s: (0, s[0])),
                pl.BlockSpec((rows, HD), lambda i, s: (0, s[0])),
                pl.BlockSpec((rows, HD), lambda i, s: (0, s[0])),
            ]
            + [piece] * len(pieces),
            out_specs=pl.BlockSpec((rows, span), lambda i, s: (0, 0)),
        ),
        out_shape=jax.ShapeDtypeStruct((rows, span), jnp.bfloat16),
        name="merge",
    )(place, mask, queries, suffix_keys, suffix_values, *pieces)


def project_kernel(order_ref, stream_ref, *refs):
    count = (len(refs) - 1) // 2
    total = stream_ref[...].astype(jnp.float32)
    for weight, piece in zip(refs[:count], refs[count : 2 * count]):
        total = total + jnp.dot(piece[...], weight[...], preferred_element_type=jnp.float32)
    refs[-1][...] = total.astype(jnp.bfloat16)


def project(order, stream, weight, pieces):
    rows, width = stream.shape
    span = pieces[0].shape[1]
    return pl.pallas_call(
        project_kernel,
        grid_spec=pltpu.PrefetchScalarGridSpec(
            num_scalar_prefetch=1,
            grid=(1,),
            in_specs=[pl.BlockSpec((rows, width), lambda i, s: (0, 0))]
            + [
                pl.BlockSpec((span, width), lambda i, s, k=k: (s[k], 0))
                for k in range(len(pieces))
            ]
            + [pl.BlockSpec((rows, span), lambda i, s: (0, 0))] * len(pieces),
            out_specs=pl.BlockSpec((rows, width), lambda i, s: (0, 0)),
        ),
        out_shape=jax.ShapeDtypeStruct((rows, width), jnp.bfloat16),
        name="project",
    )(order, stream, *[weight] * len(pieces), *pieces)


def widen_kernel(table_ref, rows_ref, gate_ref, up_ref, out_ref, acc_ref):
    step = pl.program_id(0)
    count, capacity = rows_ref.shape[:2]
    width = gate_ref.shape[2]
    filled = out_ref.shape[0] - pl.num_programs(0) * count * ROWS

    @pl.when(step == 0)
    def _():
        acc_ref[filled:, :] = jnp.zeros((acc_ref.shape[0] - filled, 2 * width), jnp.float32)

    for k in range(count):
        here = pl.ds(pl.multiple_of(table_ref[1 + step * count + k], ROWS), capacity)
        acc_ref[here, :width] = jnp.dot(
            rows_ref[k], gate_ref[k], preferred_element_type=jnp.float32
        )
        acc_ref[here, width:] = jnp.dot(
            rows_ref[k], up_ref[k], preferred_element_type=jnp.float32
        )

    @pl.when(step == pl.num_programs(0) - 1)
    def _():
        out_ref[...] = acc_ref[: out_ref.shape[0], :].astype(jnp.bfloat16)


def widen(table, rows_in, w_gate, w_up, parts, slots):
    experts, capacity, depth = rows_in.shape
    width = w_gate.shape[2] // parts
    weight = pl.BlockSpec((PER_STEP, depth, width), lambda e, s: (e, 0, s[0]))
    return pl.pallas_call(
        widen_kernel,
        grid_spec=pltpu.PrefetchScalarGridSpec(
            num_scalar_prefetch=1,
            grid=(experts // PER_STEP,),
            in_specs=[
                pl.BlockSpec((PER_STEP, capacity, depth), lambda e, s: (e, 0, 0)),
                weight,
                weight,
            ],
            out_specs=pl.BlockSpec((slots, 2 * width), lambda e, s: (0, 0)),
            scratch_shapes=[pltpu.VMEM((slots + capacity, 2 * width), jnp.float32)],
        ),
        out_shape=jax.ShapeDtypeStruct((slots, 2 * width), jnp.bfloat16),
        name="widen",
    )(table, rows_in, w_gate, w_up)


def narrow_kernel(table_ref, own_ref, far_ref, near_w_ref, far_w_ref, pick_ref, scale_ref, init_ref, out_ref, own_f, far_f):
    step = pl.program_id(0)
    slots = own_ref.shape[0]
    count, capacity = pick_ref.shape[:2]

    @pl.when(step == 0)
    def _():
        own_f[:slots, :] = own_ref[...].astype(jnp.float32)
        far_f[:slots, :] = far_ref[...].astype(jnp.float32)
        own_f[slots:, :] = jnp.zeros((capacity, own_f.shape[1]), jnp.float32)
        far_f[slots:, :] = jnp.zeros((capacity, far_f.shape[1]), jnp.float32)
        out_ref[...] = init_ref[...]

    for k in range(count):
        here = pl.ds(pl.multiple_of(table_ref[2 + step * count + k], ROWS), capacity)
        rows = jnp.dot(
            own_f[here, :].astype(jnp.bfloat16), near_w_ref[k], preferred_element_type=jnp.float32
        ) + jnp.dot(
            far_f[here, :].astype(jnp.bfloat16), far_w_ref[k], preferred_element_type=jnp.float32
        )
        rows = (rows * scale_ref[k]).astype(jnp.bfloat16)
        out_ref[...] += lax.dot_general(
            pick_ref[k], rows, (((0,), (0,)), ((), ())), preferred_element_type=jnp.float32
        )


def narrow(table, own, far, w_down, pick, scale, init):
    slots, width = own.shape
    experts, capacity, tokens = pick.shape
    cols = w_down.shape[2]
    return pl.pallas_call(
        narrow_kernel,
        grid_spec=pltpu.PrefetchScalarGridSpec(
            num_scalar_prefetch=1,
            grid=(experts // PER_STEP,),
            in_specs=[
                pl.BlockSpec((slots, width), lambda e, s: (0, 0)),
                pl.BlockSpec((slots, width), lambda e, s: (0, 0)),
                pl.BlockSpec((PER_STEP, width, cols), lambda e, s: (e, s[0], 0)),
                pl.BlockSpec((PER_STEP, width, cols), lambda e, s: (e, s[1], 0)),
                pl.BlockSpec((PER_STEP, capacity, tokens), lambda e, s: (e, 0, 0)),
                pl.BlockSpec((PER_STEP, capacity, 1), lambda e, s: (e, 0, 0)),
                pl.BlockSpec((tokens, cols), lambda e, s: (0, 0)),
            ],
            out_specs=pl.BlockSpec((tokens, cols), lambda e, s: (0, 0)),
            scratch_shapes=[
                pltpu.VMEM((slots + capacity, width), jnp.float32),
                pltpu.VMEM((slots + capacity, width), jnp.float32),
            ],
        ),
        out_shape=jax.ShapeDtypeStruct((tokens, cols), jnp.float32),
        name="narrow",
    )(table, own, far, w_down, w_down, pick, scale, init)


def take_block(value, index, size, axis):
    return lax.dynamic_slice_in_dim(value, index * size, size, axis)


def square_body(
    stream_in,
    queries,
    suffix_keys,
    suffix_values,
    prefix_keys,
    prefix_values,
    lengths,
    req_group,
    owners,
    out_proj,
    norm_gain,
    w_gate,
    w_up,
    w_down,
    routes,
    route_logits,
):
    n_gx, n_gy = 4, 8
    gx_index = lax.axis_index("gx")
    gy_index = lax.axis_index("gy")
    z_index = gy_index // 2
    core = gy_index % 2
    levels = n_gy // 2
    tok_dev = queries.shape[0]
    half_q = queries.shape[1] // 2
    half_kv = prefix_keys.shape[2] // 2
    i32 = jnp.int32
    as_vector = lambda *items: jnp.stack([jnp.asarray(item, i32) for item in items])

    mine_q = take_block(queries, core, half_q, 1)
    far_kv = flip(
        jnp.concatenate(
            [
                take_block(prefix_keys[0], 1 - core, half_kv, 1),
                take_block(prefix_values[0], 1 - core, half_kv, 1),
            ],
            axis=1,
        ),
        "gy",
        n_gy,
        1,
    )
    all_q = [mine_q] + [flip(mine_q, "gx", n_gx, b) for b in range(1, n_gx)]
    core_vec = as_vector(core)
    partial = [attend(core_vec, q, prefix_keys, prefix_values, far_kv) for q in all_q]
    pieces = [partial[0]] + [flip(partial[b], "gx", n_gx, b) for b in range(1, n_gx)]

    places = jnp.arange(tok_dev, dtype=i32)
    lens = lengths[0]
    ends = jnp.sum(
        jnp.where(jnp.arange(lens.shape[0])[:, None] >= jnp.arange(lens.shape[0])[None, :], lens[None, :], 0),
        axis=1,
    )
    requests = jnp.sum((ends[None, :] <= places[:, None]).astype(i32), axis=1)
    holders = jnp.sum(
        jnp.where(req_group[0][:, None] == jnp.arange(GROUPS, dtype=i32)[None, :], owners[None, :], 0),
        axis=1,
    )
    holder = jnp.sum(
        jnp.where(requests[:, None] == jnp.arange(lens.shape[0], dtype=i32)[None, :], holders[None, :], 0),
        axis=1,
    )
    pick = (holder ^ gx_index)[:, None]
    allowed = (
        (requests[:, None] == requests[None, :]) & (places[None, :] <= places[:, None])
    ).astype(jnp.float32)

    chosen = choose(as_vector(z_index), pick, pieces, levels)
    shares = [chosen[0]] + [flip(chosen[s], "gy", n_gy, 2 * s) for s in range(1, levels)]
    block = core * levels + z_index
    heads = merge(
        as_vector(block, z_index), allowed, queries, suffix_keys, suffix_values, shares
    )
    near = [heads] + [flip(heads, "gy", n_gy, 2 * s) for s in range(1, levels)]
    far = flip(jnp.concatenate(near, axis=1), "gy", n_gy, 1)
    span = heads.shape[1]
    features = near + [far[:, s * span : (s + 1) * span] for s in range(levels)]
    order = as_vector(
        *[core * levels + (z_index ^ s) for s in range(levels)],
        *[(1 - core) * levels + (z_index ^ s) for s in range(levels)],
    )
    resid = project(order, stream_in, out_proj, features)

    tokens = n_gx * tok_dev
    experts = w_gate.shape[0]
    capacity = tokens * 3 // 8
    slots = routes.shape[0] * routes.shape[1] + experts * ROWS
    relative = lambda table: jnp.concatenate(
        [take_block(table, gx_index ^ b, tok_dev, 0) for b in range(n_gx)], axis=0
    )
    routes_rel = relative(routes)
    weights_rel = jax.nn.softmax(relative(route_logits), axis=1)
    named = routes_rel[:, :, None] == jnp.arange(experts, dtype=i32)[None, None, :]
    hits = jnp.sum(named.astype(jnp.float32), axis=1)
    weight_of = jnp.sum(jnp.where(named, weights_rel[:, :, None], 0.0), axis=1)
    steps = jnp.arange(tokens, dtype=i32)
    before = (steps[:, None] > steps[None, :]).astype(jnp.bfloat16)
    position = jnp.dot(
        before, hits.astype(jnp.bfloat16), preferred_element_type=jnp.float32
    ).astype(i32)
    counts = jnp.sum(hits, axis=0).astype(i32)
    kinds = jnp.arange(experts, dtype=i32)
    padded = (counts + ROWS - 1) // ROWS * ROWS
    starts = jnp.sum(jnp.where(kinds[:, None] > kinds[None, :], padded[None, :], 0), axis=1)
    place_of = jnp.where(hits > 0, position, -1)
    chosen_row = place_of.T[:, None, :] == jnp.arange(capacity, dtype=i32)[None, :, None]
    row_pick = chosen_row.astype(jnp.bfloat16)
    row_weight = jnp.sum(jnp.where(chosen_row, weight_of.T[:, None, :], 0.0), axis=2)[:, :, None]

    all_resid = jnp.concatenate(
        [resid] + [flip(resid, "gx", n_gx, b) for b in range(1, n_gx)], axis=0
    ).astype(jnp.float32)
    scaled = (all_resid * norm_gain[None, :]).astype(jnp.bfloat16)
    squares = jnp.sum(all_resid * all_resid, axis=1).reshape(-1, LANES)
    rows_in = (
        jnp.dot(
            row_pick.reshape(experts * capacity, tokens),
            scaled,
            preferred_element_type=jnp.float32,
        )
        .astype(jnp.bfloat16)
        .reshape(experts, capacity, -1)
    )

    near_id = (z_index ^ (z_index >> 1)) & 1
    wrap_id = z_index >> 1
    routes_z = [((near_id, 2), (wrap_id, 6)), ((wrap_id, 6), (near_id, 2))]
    slot_of = jnp.where(hits > 0, starts[None, :] + position, -1)

    def quarter_rstd(quarter):
        row_ids = quarter * (slots // 4) + jnp.arange(slots // 4, dtype=i32)
        owner_mask = jnp.any(row_ids[:, None, None] == slot_of.T[None, :, :], axis=1)
        return jnp.sum(jnp.where(owner_mask, rstd[None, :], 0.0), axis=1, keepdims=True)

    f32 = jnp.float32
    parts = 2 * CHUNKS
    rounded = lambda a, b: (a.astype(f32) + b.astype(f32)).astype(jnp.bfloat16)
    halves = []
    for chunk in range(CHUNKS):
        (half_id, half_bit), _ = routes_z[chunk % 2]
        tables = [
            jnp.concatenate([as_vector(2 * chunk + side), starts]) for side in (1 - core, core)
        ]
        away = widen(tables[0], rows_in, w_gate, w_up, parts, slots)
        if chunk == 0:
            squares = squares + flip(squares, "gy", n_gy, 1)
        rows_in, away, squares = lax.optimization_barrier((rows_in, away, squares))
        seen = flip(away, "gy", n_gy, 1)
        keep = widen(tables[1], rows_in, w_gate, w_up, parts, slots)
        if chunk == 0:
            squares = squares + sum(flip(squares, "gy", n_gy, bit) for bit in (2, 4, 6))
        part = rounded(keep, seen)
        send = take_block(part, 1 - half_id, slots // 2, 0)
        keep = take_block(part, half_id, slots // 2, 0)
        rows_in, send, keep, squares = lax.optimization_barrier((rows_in, send, keep, squares))
        halves.append((keep, flip(send, "gy", n_gy, half_bit)))
    rstd = 1.0 / jnp.sqrt(squares.reshape(-1) / D + EPSILON)
    hidden = []
    for chunk, (keep, seen) in enumerate(halves):
        (half_id, _), (low_id, low_bit) = routes_z[chunk % 2]
        part = rounded(keep, seen)
        seen = flip(take_block(part, 1 - low_id, slots // 4, 0), "gy", n_gy, low_bit)
        part = take_block(part, low_id, slots // 4, 0).astype(f32) + seen.astype(f32)
        width = part.shape[1] // 2
        row_rstd = quarter_rstd(half_id * 2 + low_id)
        gate = part[:, :width] * row_rstd
        up = part[:, width:] * row_rstd
        hidden.append((jax.nn.silu(gate) * up).astype(jnp.bfloat16))
    total = jnp.zeros((tokens, w_down.shape[2]), f32)
    hidden[0], row_pick, row_weight, total = lax.optimization_barrier(
        (hidden[0], row_pick, row_weight, total)
    )
    for chunk, part in enumerate(hidden):
        for index, bit in routes_z[chunk % 2][::-1]:
            seen = flip(part, "gy", n_gy, bit)
            first = index == 0
            part = jnp.concatenate(
                [jnp.where(first, part, seen), jnp.where(first, seen, part)], axis=0
            )
        seen = flip(part, "gy", n_gy, 1)
        table = jnp.concatenate([as_vector(2 * chunk + core, 2 * chunk + 1 - core), starts])
        total = narrow(table, part, seen, w_down, row_pick, row_weight, total)
    total = total.astype(jnp.bfloat16)
    back = [total[:tok_dev]] + [
        flip(total[b * tok_dev : (b + 1) * tok_dev], "gx", n_gx, b) for b in range(1, n_gx)
    ]
    expert_out = sum(piece.astype(f32) for piece in back)
    return (resid.astype(f32) + expert_out).astype(jnp.bfloat16)


def fits(mesh, args):
    queries, suffix_keys, prefix_keys = args[1], args[2], args[4]
    return (
        dict(mesh.shape) == {"gx": 4, "gy": 8}
        and suffix_keys.shape[1] == 8 * HD
        and queries.shape[1] % (8 * HD) == 0
        and prefix_keys.shape[2] == 8 * HD
    )


def solution(mesh):
    placed = (
        P("gx", "gy"),
        P("gx", None),
        P("gx", None),
        P("gx", None),
        P("gx", "gy", None),
        P("gx", "gy", None),
        P("gx", None),
        P("gx", None),
        P(),
        P(None, "gy"),
        P("gy"),
        P(None, "gy", "gx"),
        P(None, "gy", "gx"),
        P(None, "gx", "gy"),
        P(),
        P(),
    )

    def run(*args):
        chosen = square_body if fits(mesh, args) else body
        return jax.shard_map(
            chosen, mesh=mesh, in_specs=placed, out_specs=P("gx", "gy"), check_vma=False
        )(*args)

    return run
```

```python
import math

import jax
import jax.numpy as jnp
from jax import lax
from jax.experimental import pallas as pl
from jax.experimental.pallas import tpu as pltpu
from jax.sharding import PartitionSpec as P

D = 4096
HD = 128
GROUPS = 3
LANES = 128
ROWS = 8
PER_STEP = 2
CHUNKS = 2


NEGATIVE = -1e30
EPSILON = 1e-05


def spread(value, axis, source):
    kept = jnp.where(lax.axis_index(axis) == source, value, 0).astype(value.dtype)
    return lax.psum(kept, axis)


def combined_all(value, axis, join):
    pieces = jax.tree.map(lambda part: lax.all_gather(part, axis), value)
    head = jax.tree.map(lambda part: part[0], pieces)
    tail = jax.tree.map(lambda part: part[1:], pieces)
    total, _ = lax.scan(lambda total, section: (join(total, section), None), head, tail)
    return total


def combine_parts(first, second):
    first_max, first_total, first_acc = first
    second_max, second_total, second_acc = second
    joined = jnp.maximum(first_max, second_max)
    first_factor = jnp.exp(first_max - joined)
    second_factor = jnp.exp(second_max - joined)
    return (
        joined,
        first_total * first_factor + second_total * second_factor,
        first_acc * first_factor[..., None] + second_acc * second_factor[..., None],
    )


def body(
    stream_in,
    queries,
    suffix_keys,
    suffix_values,
    prefix_keys,
    prefix_values,
    lengths,
    req_group,
    owners,
    out_proj,
    norm_gain,
    w_gate,
    w_up,
    w_down,
    routes,
    route_logits,
):
    highest = lax.Precision.HIGHEST
    tok_dev = queries.shape[0]
    kv_heads = suffix_keys.shape[1] // HD
    per_kv = queries.shape[1] // suffix_keys.shape[1]
    scaling = 1.0 / math.sqrt(HD)
    gy_index = lax.axis_index("gy")
    places = jnp.arange(tok_dev, dtype=jnp.int32)
    ends = jnp.cumsum(lengths[0])
    requests = jnp.sum((ends[None, :] <= places[:, None]).astype(jnp.int32), axis=1)
    picks = (requests[:, None] == jnp.arange(ends.shape[0], dtype=jnp.int32)[None, :]).astype(
        jnp.int32
    )
    group_ids = jnp.sum(picks * req_group[0][None, :], axis=1)
    query_blocks = queries.reshape(tok_dev, kv_heads, per_kv, HD)
    allowed = (
        (requests[:, None] == requests[None, :])
        & (places[None, :] <= places[:, None])
        & (gy_index == 0)
    )
    suffix_k = suffix_keys.reshape(tok_dev, kv_heads, HD)
    suffix_v = suffix_values.reshape(tok_dev, kv_heads, HD)
    suffix_scores = (
        jnp.einsum("tcqd,scd->tcqs", query_blocks, suffix_k, preferred_element_type=jnp.float32)
        * scaling
    )
    suffix_masked = jnp.where(allowed[:, None, None, :], suffix_scores, NEGATIVE)
    slab_rows = prefix_keys.shape[1]
    score_init = jnp.full((GROUPS, tok_dev, kv_heads, per_kv, slab_rows), NEGATIVE, jnp.float32)
    value_init = jnp.zeros((GROUPS, slab_rows, kv_heads, HD), prefix_values.dtype)

    def one_group(group_id, carry):
        score_stack, value_stack = carry
        holder = lax.dynamic_index_in_dim(owners, group_id, 0, keepdims=False)
        slab_keys, slab_values = (
            spread(prefix_keys[0], "gx", holder),
            spread(prefix_values[0], "gx", holder),
        )
        slab_keys = slab_keys.reshape(-1, kv_heads, HD)
        group_scores = (
            jnp.einsum(
                "tcqd,pcd->tcqp", query_blocks, slab_keys, preferred_element_type=jnp.float32
            )
            * scaling
        )
        masked = jnp.where((group_ids == group_id)[:, None, None, None], group_scores, NEGATIVE)
        score_stack = lax.dynamic_update_index_in_dim(score_stack, masked, group_id, 0)
        value_stack = lax.dynamic_update_index_in_dim(
            value_stack, slab_values.reshape(-1, kv_heads, HD), group_id, 0
        )
        return (score_stack, value_stack)

    score_stack, value_stack = lax.fori_loop(0, GROUPS, one_group, (score_init, value_init))
    prefix_scores = jnp.moveaxis(score_stack, 0, 3).reshape(
        tok_dev, kv_heads, per_kv, GROUPS * slab_rows
    )
    all_scores = jnp.concatenate([suffix_masked, prefix_scores], axis=3)
    all_values = jnp.concatenate(
        [suffix_v, value_stack.reshape(GROUPS * slab_rows, kv_heads, HD)], axis=0
    ).astype(jnp.float32)
    local_max = jnp.max(all_scores, axis=3)
    probs = jnp.exp(all_scores - local_max[..., None])
    local_total = jnp.sum(probs, axis=3)
    local_acc = jnp.einsum("tcqp,pcd->tcqd", probs, all_values, precision=highest)
    merged_max, merged_total, merged_acc = combined_all(
        (local_max, local_total, local_acc), "gy", combine_parts
    )
    attention = (merged_acc / merged_total[..., None]).reshape(tok_dev, -1).astype(jnp.bfloat16)
    resid = (
        stream_in.astype(jnp.float32)
        + jnp.dot(attention, out_proj, preferred_element_type=jnp.float32)
    ).astype(jnp.bfloat16)
    resid_all = lax.all_gather(resid, "gx", axis=0, tiled=True)
    resid_all_f = resid_all.astype(jnp.float32)
    scaled_all = (resid_all_f * norm_gain[None, :]).astype(jnp.bfloat16)
    squares_all = jnp.sum(resid_all_f * resid_all_f, axis=1)
    tokens = resid_all.shape[0]
    experts = w_gate.shape[0]
    width = w_gate.shape[2]
    top_count = routes.shape[1]
    capacity = tokens * 3 // 8
    flat_routes = routes.reshape(-1)
    onehot = (flat_routes[:, None] == jnp.arange(experts, dtype=jnp.int32)[None, :]).astype(
        jnp.int32
    )
    earlier = jnp.cumsum(onehot, axis=0) - onehot
    position = jnp.sum(earlier * onehot, axis=1)
    slot_of_pair = flat_routes * capacity + position
    pair_token = jnp.arange(flat_routes.shape[0], dtype=jnp.int32) // top_count
    matches = slot_of_pair[:, None] == jnp.arange(experts * capacity, dtype=jnp.int32)[None, :]
    slot_token = jnp.sum(jnp.where(matches, pair_token[:, None], 0), axis=0)
    pair_weight = jax.nn.softmax(route_logits, axis=1)
    slot_pairs = slot_of_pair.reshape(tokens, top_count)
    rows_in = jnp.take(scaled_all, slot_token, axis=0).reshape(experts, capacity, -1)
    squares_in = jnp.take(squares_all, slot_token)
    gate_part = jnp.einsum(
        "ecd,edf->ecf", rows_in, w_gate, preferred_element_type=jnp.float32
    ).reshape(experts * capacity, width)
    up_part = jnp.einsum("ecd,edf->ecf", rows_in, w_up, preferred_element_type=jnp.float32).reshape(
        experts * capacity, width
    )
    gate_sum, up_sum, square_sum = lax.psum((gate_part, up_part, squares_in), "gy")
    inverse = 1.0 / jnp.sqrt(square_sum / D + EPSILON)
    hidden = (jax.nn.silu(gate_sum * inverse[:, None]) * (up_sum * inverse[:, None])).astype(
        jnp.bfloat16
    )
    expert_rows = jnp.einsum(
        "ecf,efd->ecd",
        hidden.reshape(experts, capacity, width),
        w_down,
        preferred_element_type=jnp.float32,
    ).reshape(experts * capacity, -1)
    picked = jnp.take(expert_rows, slot_pairs, axis=0)
    expert_out = lax.psum_scatter(
        jnp.sum(picked * pair_weight[..., None], axis=1).astype(jnp.bfloat16),
        "gx",
        scatter_dimension=0,
        tiled=True,
    ).astype(jnp.float32)
    return (resid.astype(jnp.float32) + expert_out).astype(jnp.bfloat16)


def flip(value, axis, size, bit):
    return lax.ppermute(value, axis, [(i, i ^ bit) for i in range(size)])


def attend_kernel(core_ref, q_ref, k_own_ref, v_own_ref, k_far_ref, v_far_ref, out_ref):
    step = pl.program_id(0)
    count = k_far_ref.shape[1] // HD
    per_kv = q_ref.shape[1] // HD // count
    rows = q_ref.shape[0]
    scaling = 1.0 / math.sqrt(HD)
    factor = scaling * math.log2(math.e)
    contract = (((1,), (1,)), ((), ()))
    lanes = lax.broadcasted_iota(jnp.int32, (rows, LANES), 1)
    heads = pl.num_programs(0) * count * per_kv
    stats = jnp.zeros((rows, LANES), jnp.float32)
    for c in range(count):
        cols = slice(c * HD, (c + 1) * HD)
        q = jnp.concatenate(
            [q_ref[:, j * HD : (j + 1) * HD] for j in range(c * per_kv, (c + 1) * per_kv)], axis=0
        )
        near = lax.dot_general(q, k_own_ref[0, :, cols], contract, preferred_element_type=jnp.float32)
        far = lax.dot_general(q, k_far_ref[:, cols], contract, preferred_element_type=jnp.float32)
        top = jnp.maximum(
            jnp.max(near, axis=1, keepdims=True), jnp.max(far, axis=1, keepdims=True)
        )
        near = jnp.exp2((near - top) * factor)
        far = jnp.exp2((far - top) * factor)
        total = jnp.sum(near, axis=1, keepdims=True) + jnp.sum(far, axis=1, keepdims=True)
        acc = jnp.dot(
            near.astype(jnp.bfloat16), v_own_ref[0, :, cols], preferred_element_type=jnp.float32
        ) + jnp.dot(
            far.astype(jnp.bfloat16), v_far_ref[:, cols], preferred_element_type=jnp.float32
        )
        acc = acc / total
        lse = top * scaling + jnp.log(total)
        for j in range(per_kv):
            part = lse[j * rows : (j + 1) * rows]
            high = part.astype(jnp.bfloat16).astype(jnp.float32)
            middle = (part - high).astype(jnp.bfloat16).astype(jnp.float32)
            low = part - high - middle
            place = (step * count + c) * per_kv + j
            stats = jnp.where(lanes == place, high, stats)
            stats = jnp.where(lanes == heads + place, middle, stats)
            stats = jnp.where(lanes == 2 * heads + place, low, stats)
            where = pl.multiple_of(place * HD, HD)
            out_ref[:, pl.ds(where, HD)] = acc[j * rows : (j + 1) * rows].astype(jnp.bfloat16)
    width = out_ref.shape[1] - LANES

    @pl.when(step == 0)
    def _():
        out_ref[:, width:] = stats.astype(jnp.bfloat16)

    @pl.when(step > 0)
    def _():
        out_ref[:, width:] = (out_ref[:, width:].astype(jnp.float32) + stats).astype(jnp.bfloat16)


def attend(core, q, keys, values, far):
    rows, width = q.shape
    slab = keys.shape[1]
    heads = far.shape[1] // 2 // HD
    steps = heads // PER_STEP
    span = width // steps
    depth = PER_STEP * HD
    return pl.pallas_call(
        attend_kernel,
        grid_spec=pltpu.PrefetchScalarGridSpec(
            num_scalar_prefetch=1,
            grid=(steps,),
            in_specs=[
                pl.BlockSpec((rows, span), lambda h, s: (0, h)),
                pl.BlockSpec((1, slab, depth), lambda h, s: (0, 0, s[0] * steps + h)),
                pl.BlockSpec((1, slab, depth), lambda h, s: (0, 0, s[0] * steps + h)),
                pl.BlockSpec((slab, depth), lambda h, s: (0, h)),
                pl.BlockSpec((slab, depth), lambda h, s: (0, steps + h)),
            ],
            out_specs=pl.BlockSpec((rows, width + LANES), lambda h, s: (0, 0)),
        ),
        out_shape=jax.ShapeDtypeStruct((rows, width + LANES), jnp.bfloat16),
        name="attend",
    )(core, q, keys, values, far, far)


def choose_kernel(z_ref, pick_ref, a_ref, b_ref, c_ref, d_ref, *outs):
    pick = pick_ref[...]
    width = a_ref.shape[1] - LANES
    span = outs[0].shape[1] - LANES

    def chosen(where, size):
        first = jnp.where(pick == 1, b_ref[:, where].astype(jnp.float32), a_ref[:, where].astype(jnp.float32))
        second = jnp.where(pick == 3, d_ref[:, where].astype(jnp.float32), c_ref[:, where].astype(jnp.float32))
        return jnp.where(pick >= 2, second, first).astype(jnp.bfloat16)

    stats = chosen(pl.ds(width, LANES), LANES)
    for s, out in enumerate(outs):
        start = pl.multiple_of((z_ref[0] ^ s) * span, LANES)
        out[:, :span] = chosen(pl.ds(start, span), span)
        out[:, span:] = stats


def choose(z, pick, pieces, count):
    rows, width = pieces[0].shape
    span = (width - LANES) // count
    shape = jax.ShapeDtypeStruct((rows, span + LANES), jnp.bfloat16)
    whole = pl.BlockSpec((rows, width), lambda i, s: (0, 0))
    return pl.pallas_call(
        choose_kernel,
        grid_spec=pltpu.PrefetchScalarGridSpec(
            num_scalar_prefetch=1,
            grid=(1,),
            in_specs=[pl.BlockSpec((rows, 1), lambda i, s: (0, 0))] + [whole] * 4,
            out_specs=[pl.BlockSpec((rows, span + LANES), lambda i, s: (0, 0))] * count,
        ),
        out_shape=[shape] * count,
        name="choose",
    )(z, pick, *pieces)


def merge_kernel(place_ref, mask_ref, q_ref, k_ref, v_ref, *refs):
    pieces, out_ref = refs[:-1], refs[-1]
    per_kv = q_ref.shape[1] // HD
    heads = per_kv * len(pieces)
    scaling = 1.0 / math.sqrt(HD)
    allowed = mask_ref[...] > 0
    lanes = lax.broadcasted_iota(jnp.int32, (q_ref.shape[0], LANES), 1)
    stats = [piece[:, per_kv * HD :].astype(jnp.float32) for piece in pieces]
    for j in range(per_kv):
        cols = slice(j * HD, (j + 1) * HD)
        scores = (
            lax.dot_general(
                q_ref[:, cols],
                k_ref[...],
                (((1,), (1,)), ((), ())),
                preferred_element_type=jnp.float32,
            )
            * scaling
        )
        scores = jnp.where(allowed, scores, NEGATIVE)
        top = jnp.max(scores, axis=1, keepdims=True)
        probs = jnp.exp(scores - top)
        base = place_ref[1] * per_kv + j
        mine = (lanes == base) | (lanes == heads + base) | (lanes == 2 * heads + base)
        sizes = [jnp.sum(jnp.where(mine, part, 0.0), axis=1, keepdims=True) for part in stats]
        peak = top
        for size in sizes:
            peak = jnp.maximum(peak, size)
        share = jnp.exp(top - peak)
        total = jnp.sum(probs, axis=1, keepdims=True) * share
        acc = (
            jnp.dot(probs.astype(jnp.bfloat16), v_ref[...], preferred_element_type=jnp.float32)
            * share
        )
        for size, piece in zip(sizes, pieces):
            weight = jnp.exp(size - peak)
            total = total + weight
            acc = acc + weight * piece[:, cols].astype(jnp.float32)
        out_ref[:, cols] = (acc / total).astype(jnp.bfloat16)


def merge(place, mask, queries, suffix_keys, suffix_values, pieces):
    rows = queries.shape[0]
    span = pieces[0].shape[1] - LANES
    piece = pl.BlockSpec((rows, span + LANES), lambda i, s: (0, 0))
    return pl.pallas_call(
        merge_kernel,
        grid_spec=pltpu.PrefetchScalarGridSpec(
            num_scalar_prefetch=1,
            grid=(1,),
            in_specs=[
                pl.BlockSpec((rows, rows), lambda i, s: (0, 0)),
                pl.BlockSpec((rows, span), lambda i, s: (0, s[0])),
                pl.BlockSpec((rows, HD), lambda i, s: (0, s[0])),
                pl.BlockSpec((rows, HD), lambda i, s: (0, s[0])),
            ]
            + [piece] * len(pieces),
            out_specs=pl.BlockSpec((rows, span), lambda i, s: (0, 0)),
        ),
        out_shape=jax.ShapeDtypeStruct((rows, span), jnp.bfloat16),
        name="merge",
    )(place, mask, queries, suffix_keys, suffix_values, *pieces)


def project_kernel(order_ref, stream_ref, *refs):
    count = (len(refs) - 1) // 2
    total = stream_ref[...].astype(jnp.float32)
    for weight, piece in zip(refs[:count], refs[count : 2 * count]):
        total = total + jnp.dot(piece[...], weight[...], preferred_element_type=jnp.float32)
    refs[-1][...] = total.astype(jnp.bfloat16)


def project(order, stream, weight, pieces):
    rows, width = stream.shape
    span = pieces[0].shape[1]
    return pl.pallas_call(
        project_kernel,
        grid_spec=pltpu.PrefetchScalarGridSpec(
            num_scalar_prefetch=1,
            grid=(1,),
            in_specs=[pl.BlockSpec((rows, width), lambda i, s: (0, 0))]
            + [
                pl.BlockSpec((span, width), lambda i, s, k=k: (s[k], 0))
                for k in range(len(pieces))
            ]
            + [pl.BlockSpec((rows, span), lambda i, s: (0, 0))] * len(pieces),
            out_specs=pl.BlockSpec((rows, width), lambda i, s: (0, 0)),
        ),
        out_shape=jax.ShapeDtypeStruct((rows, width), jnp.bfloat16),
        name="project",
    )(order, stream, *[weight] * len(pieces), *pieces)


def widen_kernel(table_ref, rows_ref, gate_ref, up_ref, out_ref, acc_ref):
    step = pl.program_id(0)
    count, capacity = rows_ref.shape[:2]
    width = gate_ref.shape[2]
    filled = out_ref.shape[0] - pl.num_programs(0) * count * ROWS

    @pl.when(step == 0)
    def _():
        acc_ref[filled:, :] = jnp.zeros((acc_ref.shape[0] - filled, 2 * width), jnp.float32)

    for k in range(count):
        here = pl.ds(pl.multiple_of(table_ref[1 + step * count + k], ROWS), capacity)
        acc_ref[here, :width] = jnp.dot(
            rows_ref[k], gate_ref[k], preferred_element_type=jnp.float32
        )
        acc_ref[here, width:] = jnp.dot(
            rows_ref[k], up_ref[k], preferred_element_type=jnp.float32
        )

    @pl.when(step == pl.num_programs(0) - 1)
    def _():
        out_ref[...] = acc_ref[: out_ref.shape[0], :].astype(jnp.bfloat16)


def widen(table, rows_in, w_gate, w_up, parts, slots):
    experts, capacity, depth = rows_in.shape
    width = w_gate.shape[2] // parts
    weight = pl.BlockSpec((PER_STEP, depth, width), lambda e, s: (e, 0, s[0]))
    return pl.pallas_call(
        widen_kernel,
        grid_spec=pltpu.PrefetchScalarGridSpec(
            num_scalar_prefetch=1,
            grid=(experts // PER_STEP,),
            in_specs=[
                pl.BlockSpec((PER_STEP, capacity, depth), lambda e, s: (e, 0, 0)),
                weight,
                weight,
            ],
            out_specs=pl.BlockSpec((slots, 2 * width), lambda e, s: (0, 0)),
            scratch_shapes=[pltpu.VMEM((slots + capacity, 2 * width), jnp.float32)],
        ),
        out_shape=jax.ShapeDtypeStruct((slots, 2 * width), jnp.bfloat16),
        name="widen",
    )(table, rows_in, w_gate, w_up)


def narrow_kernel(table_ref, own_ref, far_ref, near_w_ref, far_w_ref, pick_ref, scale_ref, init_ref, out_ref, own_f, far_f):
    step = pl.program_id(0)
    slots = own_ref.shape[0]
    count, capacity = pick_ref.shape[:2]

    @pl.when(step == 0)
    def _():
        own_f[:slots, :] = own_ref[...].astype(jnp.float32)
        far_f[:slots, :] = far_ref[...].astype(jnp.float32)
        own_f[slots:, :] = jnp.zeros((capacity, own_f.shape[1]), jnp.float32)
        far_f[slots:, :] = jnp.zeros((capacity, far_f.shape[1]), jnp.float32)
        out_ref[...] = init_ref[...]

    for k in range(count):
        here = pl.ds(pl.multiple_of(table_ref[2 + step * count + k], ROWS), capacity)
        rows = jnp.dot(
            own_f[here, :].astype(jnp.bfloat16), near_w_ref[k], preferred_element_type=jnp.float32
        ) + jnp.dot(
            far_f[here, :].astype(jnp.bfloat16), far_w_ref[k], preferred_element_type=jnp.float32
        )
        rows = (rows * scale_ref[k]).astype(jnp.bfloat16)
        out_ref[...] += lax.dot_general(
            pick_ref[k], rows, (((0,), (0,)), ((), ())), preferred_element_type=jnp.float32
        )


def narrow(table, own, far, w_down, pick, scale, init):
    slots, width = own.shape
    experts, capacity, tokens = pick.shape
    cols = w_down.shape[2]
    return pl.pallas_call(
        narrow_kernel,
        grid_spec=pltpu.PrefetchScalarGridSpec(
            num_scalar_prefetch=1,
            grid=(experts // PER_STEP,),
            in_specs=[
                pl.BlockSpec((slots, width), lambda e, s: (0, 0)),
                pl.BlockSpec((slots, width), lambda e, s: (0, 0)),
                pl.BlockSpec((PER_STEP, width, cols), lambda e, s: (e, s[0], 0)),
                pl.BlockSpec((PER_STEP, width, cols), lambda e, s: (e, s[1], 0)),
                pl.BlockSpec((PER_STEP, capacity, tokens), lambda e, s: (e, 0, 0)),
                pl.BlockSpec((PER_STEP, capacity, 1), lambda e, s: (e, 0, 0)),
                pl.BlockSpec((tokens, cols), lambda e, s: (0, 0)),
            ],
            out_specs=pl.BlockSpec((tokens, cols), lambda e, s: (0, 0)),
            scratch_shapes=[
                pltpu.VMEM((slots + capacity, width), jnp.float32),
                pltpu.VMEM((slots + capacity, width), jnp.float32),
            ],
        ),
        out_shape=jax.ShapeDtypeStruct((tokens, cols), jnp.float32),
        name="narrow",
    )(table, own, far, w_down, w_down, pick, scale, init)


def take_block(value, index, size, axis):
    return lax.dynamic_slice_in_dim(value, index * size, size, axis)


def square_body(
    stream_in,
    queries,
    suffix_keys,
    suffix_values,
    prefix_keys,
    prefix_values,
    lengths,
    req_group,
    owners,
    out_proj,
    norm_gain,
    w_gate,
    w_up,
    w_down,
    routes,
    route_logits,
):
    n_gx, n_gy = 4, 8
    gx_index = lax.axis_index("gx")
    gy_index = lax.axis_index("gy")
    z_index = gy_index // 2
    core = gy_index % 2
    levels = n_gy // 2
    tok_dev = queries.shape[0]
    half_q = queries.shape[1] // 2
    half_kv = prefix_keys.shape[2] // 2
    i32 = jnp.int32
    as_vector = lambda *items: jnp.stack([jnp.asarray(item, i32) for item in items])

    mine_q = take_block(queries, core, half_q, 1)
    far_kv = flip(
        jnp.concatenate(
            [
                take_block(prefix_keys[0], 1 - core, half_kv, 1),
                take_block(prefix_values[0], 1 - core, half_kv, 1),
            ],
            axis=1,
        ),
        "gy",
        n_gy,
        1,
    )
    all_q = [mine_q] + [flip(mine_q, "gx", n_gx, b) for b in range(1, n_gx)]
    core_vec = as_vector(core)
    partial = [attend(core_vec, q, prefix_keys, prefix_values, far_kv) for q in all_q]
    pieces = [partial[0]] + [flip(partial[b], "gx", n_gx, b) for b in range(1, n_gx)]

    places = jnp.arange(tok_dev, dtype=i32)
    lens = lengths[0]
    ends = jnp.sum(
        jnp.where(jnp.arange(lens.shape[0])[:, None] >= jnp.arange(lens.shape[0])[None, :], lens[None, :], 0),
        axis=1,
    )
    requests = jnp.sum((ends[None, :] <= places[:, None]).astype(i32), axis=1)
    holders = jnp.sum(
        jnp.where(req_group[0][:, None] == jnp.arange(GROUPS, dtype=i32)[None, :], owners[None, :], 0),
        axis=1,
    )
    holder = jnp.sum(
        jnp.where(requests[:, None] == jnp.arange(lens.shape[0], dtype=i32)[None, :], holders[None, :], 0),
        axis=1,
    )
    pick = (holder ^ gx_index)[:, None]
    allowed = (
        (requests[:, None] == requests[None, :]) & (places[None, :] <= places[:, None])
    ).astype(jnp.float32)

    chosen = choose(as_vector(z_index), pick, pieces, levels)
    shares = [chosen[0]] + [flip(chosen[s], "gy", n_gy, 2 * s) for s in range(1, levels)]
    block = core * levels + z_index
    heads = merge(
        as_vector(block, z_index), allowed, queries, suffix_keys, suffix_values, shares
    )
    near = [heads] + [flip(heads, "gy", n_gy, 2 * s) for s in range(1, levels)]
    far = flip(jnp.concatenate(near, axis=1), "gy", n_gy, 1)
    span = heads.shape[1]
    features = near + [far[:, s * span : (s + 1) * span] for s in range(levels)]
    order = as_vector(
        *[core * levels + (z_index ^ s) for s in range(levels)],
        *[(1 - core) * levels + (z_index ^ s) for s in range(levels)],
    )
    resid = project(order, stream_in, out_proj, features)

    tokens = n_gx * tok_dev
    experts = w_gate.shape[0]
    capacity = tokens * 3 // 8
    slots = routes.shape[0] * routes.shape[1] + experts * ROWS
    relative = lambda table: jnp.concatenate(
        [take_block(table, gx_index ^ b, tok_dev, 0) for b in range(n_gx)], axis=0
    )
    routes_rel = relative(routes)
    weights_rel = jax.nn.softmax(relative(route_logits), axis=1)
    named = routes_rel[:, :, None] == jnp.arange(experts, dtype=i32)[None, None, :]
    hits = jnp.sum(named.astype(jnp.float32), axis=1)
    weight_of = jnp.sum(jnp.where(named, weights_rel[:, :, None], 0.0), axis=1)
    steps = jnp.arange(tokens, dtype=i32)
    before = (steps[:, None] > steps[None, :]).astype(jnp.bfloat16)
    position = jnp.dot(
        before, hits.astype(jnp.bfloat16), preferred_element_type=jnp.float32
    ).astype(i32)
    counts = jnp.sum(hits, axis=0).astype(i32)
    kinds = jnp.arange(experts, dtype=i32)
    padded = (counts + ROWS - 1) // ROWS * ROWS
    starts = jnp.sum(jnp.where(kinds[:, None] > kinds[None, :], padded[None, :], 0), axis=1)
    place_of = jnp.where(hits > 0, position, -1)
    chosen_row = place_of.T[:, None, :] == jnp.arange(capacity, dtype=i32)[None, :, None]
    row_pick = chosen_row.astype(jnp.bfloat16)
    row_weight = jnp.sum(jnp.where(chosen_row, weight_of.T[:, None, :], 0.0), axis=2)[:, :, None]

    all_resid = jnp.concatenate(
        [resid] + [flip(resid, "gx", n_gx, b) for b in range(1, n_gx)], axis=0
    ).astype(jnp.float32)
    scaled = (all_resid * norm_gain[None, :]).astype(jnp.bfloat16)
    squares = jnp.sum(all_resid * all_resid, axis=1).reshape(-1, LANES)
    rows_in = (
        jnp.dot(
            row_pick.reshape(experts * capacity, tokens),
            scaled,
            preferred_element_type=jnp.float32,
        )
        .astype(jnp.bfloat16)
        .reshape(experts, capacity, -1)
    )

    routes_z = [((z_index & 1, 2), (z_index >> 1, 4))] * 2
    slot_of = jnp.where(hits > 0, starts[None, :] + position, -1)

    def quarter_rstd(quarter):
        row_ids = quarter * (slots // 4) + jnp.arange(slots // 4, dtype=i32)
        owner_mask = jnp.any(row_ids[:, None, None] == slot_of.T[None, :, :], axis=1)
        return jnp.sum(jnp.where(owner_mask, rstd[None, :], 0.0), axis=1, keepdims=True)

    f32 = jnp.float32
    parts = 2 * CHUNKS
    rounded = lambda a, b: (a.astype(f32) + b.astype(f32)).astype(jnp.bfloat16)
    halves = []
    for chunk in range(CHUNKS):
        (half_id, half_bit), _ = routes_z[chunk % 2]
        tables = [
            jnp.concatenate([as_vector(2 * chunk + side), starts]) for side in (1 - core, core)
        ]
        away = widen(tables[0], rows_in, w_gate, w_up, parts, slots)
        if chunk == 0:
            squares = squares + flip(squares, "gy", n_gy, 1)
        rows_in, away, squares = lax.optimization_barrier((rows_in, away, squares))
        seen = flip(away, "gy", n_gy, 1)
        keep = widen(tables[1], rows_in, w_gate, w_up, parts, slots)
        if chunk == 0:
            squares = squares + sum(flip(squares, "gy", n_gy, bit) for bit in (2, 4, 6))
        part = rounded(keep, seen)
        send = take_block(part, 1 - half_id, slots // 2, 0)
        keep = take_block(part, half_id, slots // 2, 0)
        rows_in, send, keep, squares = lax.optimization_barrier((rows_in, send, keep, squares))
        halves.append((keep, flip(send, "gy", n_gy, half_bit)))
    rstd = 1.0 / jnp.sqrt(squares.reshape(-1) / D + EPSILON)
    hidden = []
    for chunk, (keep, seen) in enumerate(halves):
        (half_id, _), (low_id, low_bit) = routes_z[chunk % 2]
        part = rounded(keep, seen)
        seen = flip(take_block(part, 1 - low_id, slots // 4, 0), "gy", n_gy, low_bit)
        part = take_block(part, low_id, slots // 4, 0).astype(f32) + seen.astype(f32)
        width = part.shape[1] // 2
        row_rstd = quarter_rstd(half_id * 2 + low_id)
        gate = part[:, :width] * row_rstd
        up = part[:, width:] * row_rstd
        hidden.append((jax.nn.silu(gate) * up).astype(jnp.bfloat16))
    total = jnp.zeros((tokens, w_down.shape[2]), f32)
    hidden[0], row_pick, row_weight, total = lax.optimization_barrier(
        (hidden[0], row_pick, row_weight, total)
    )
    for chunk, part in enumerate(hidden):
        for index, bit in routes_z[chunk % 2][::-1]:
            seen = flip(part, "gy", n_gy, bit)
            first = index == 0
            part = jnp.concatenate(
                [jnp.where(first, part, seen), jnp.where(first, seen, part)], axis=0
            )
        seen = flip(part, "gy", n_gy, 1)
        table = jnp.concatenate([as_vector(2 * chunk + core, 2 * chunk + 1 - core), starts])
        total = narrow(table, part, seen, w_down, row_pick, row_weight, total)
    total = total.astype(jnp.bfloat16)
    back = [total[:tok_dev]] + [
        flip(total[b * tok_dev : (b + 1) * tok_dev], "gx", n_gx, b) for b in range(1, n_gx)
    ]
    expert_out = sum(piece.astype(f32) for piece in back)
    return (resid.astype(f32) + expert_out).astype(jnp.bfloat16)


def fits(mesh, args):
    queries, suffix_keys, prefix_keys = args[1], args[2], args[4]
    return (
        dict(mesh.shape) == {"gx": 4, "gy": 8}
        and suffix_keys.shape[1] == 8 * HD
        and queries.shape[1] % (8 * HD) == 0
        and prefix_keys.shape[2] == 8 * HD
    )


def solution(mesh):
    placed = (
        P("gx", "gy"),
        P("gx", None),
        P("gx", None),
        P("gx", None),
        P("gx", "gy", None),
        P("gx", "gy", None),
        P("gx", None),
        P("gx", None),
        P(),
        P(None, "gy"),
        P("gy"),
        P(None, "gy", "gx"),
        P(None, "gy", "gx"),
        P(None, "gx", "gy"),
        P(),
        P(),
    )

    def run(*args):
        chosen = square_body if fits(mesh, args) else body
        return jax.shard_map(
            chosen, mesh=mesh, in_specs=placed, out_specs=P("gx", "gy"), check_vma=False
        )(*args)

    return run
```
